256 devices in a mesh: ctx: 16 (over z, x_lo), seq: 16 (over y, x_hi, core).
Axes of the slice: x: 4 (x_hi: 2, x_lo: 2; x = x_hi * 2 + x_lo), y: 4, z: 8, core: 2. Of those that a mesh axis runs over, the one named last changes fastest.
Arguments:
- normed_hidden_input: bfloat16 [16, 2048, 4096], P('seq', 'ctx'), may hold values from -6 to 6
- frozen_query_base: bfloat16 [16, 2048, 2048], P('seq', 'ctx'), may hold values from -6 to 6
- key_head_states: bfloat16 [16, 2048, 512], P('seq', 'ctx'), may hold values from -6 to 6
- value_head_states: bfloat16 [16, 2048, 512], P('seq', 'ctx'), may hold values from -6 to 6
- document_numbers: int32 [16, 2048], P('seq', 'ctx'), may hold values from 0 to 3, as said below
- tenant_block_entry: int32 [16, 64], P('seq', 'ctx'), may hold values from 0 to 5
- sequence_adapter_list: int32 [16, 6], replicated, may hold values from 0 to 15, as said below
- adapter_down_weight: bfloat16 [16, 64, 4096], P('seq', None, 'ctx'), may hold values from -0.09375 to 0.09375
- adapter_up_weight: bfloat16 [16, 64, 2048], P('seq', None, 'ctx'), may hold values from -0.75 to 0.75
- output_gradient: bfloat16 [16, 2048, 2048], P('seq', 'ctx'), may hold values from -6 to 6
Outputs:
- attention_out: bfloat16 [16, 2048, 2048], P('seq', 'ctx')
- key_grad: float32 [16, 2048, 512], P('seq', 'ctx')
- value_grad: float32 [16, 2048, 512], P('seq', 'ctx')
- down_grad: float32 [16, 64, 4096], P('seq', None, 'ctx')
- up_grad: float32 [16, 64, 2048], P('seq', None, 'ctx')
The draws below stay inside these ranges and needn't reach their ends.
Inputs may be any that keep to these rules, and one draw needn't show every extreme that they name: `document_numbers`: each sequence is cut into 4 documents of consecutive positions, numbered in order; every document starts at an even position and has 2 or more positions. `sequence_adapter_list`: each row lists 6 different tenants.
All inputs are finite; a program needn't handle non-finite values.
Results may differ from the reference program's by a relative error of at most 0.04.
Values may be sent and summed in bfloat16 or wider, within the bound.
A program may use at most 128 MiB of HBM per device.

```python
import math
import jax
import jax.numpy as jnp
import numpy as np
from jax import lax

MODEL_WIDTH = 4096
QUERY_HEADS = 16
KEY_VALUE_HEADS = 4
HEAD_SIZE = 128
ADAPTER_RANK = 64
TB = 32
PACKED_DOCUMENTS = 4
TENANT_COUNT = 16
PICK = 6
PACKED_SEQUENCES = 16
SEQUENCE_LENGTH = 2048
NBLK = 64


def document_cuts(key):
    base_key = jax.random.fold_in(key, 101)

    def one_row(row_key):
        shuffled = jax.random.permutation(row_key, SEQUENCE_LENGTH // 2 - 1).astype(jnp.int32)
        return 2 * (shuffled[:PACKED_DOCUMENTS - 1] + 1)
    return jax.vmap(one_row)(jax.random.split(base_key, PACKED_SEQUENCES))


def draw_document_numbers(key, part):
    doc_cuts = document_cuts(key)
    positions = jnp.arange(SEQUENCE_LENGTH, dtype=jnp.int32)
    return jnp.sum((doc_cuts[:, None, :] <= positions[None, :, None]).astype(jnp.int32), axis=2).astype(jnp.int32)


def draw_frozen_query_base(key, part):
    value_entries = jnp.clip(jax.random.normal(jax.random.fold_in(key, 303), (PACKED_SEQUENCES, SEQUENCE_LENGTH, QUERY_HEADS * HEAD_SIZE), jnp.float32), -6.0, 6.0)
    return value_entries.astype(jnp.bfloat16)


def draw_key_head_states(key, part):
    value_entries = jnp.clip(jax.random.normal(jax.random.fold_in(key, 404), (PACKED_SEQUENCES, SEQUENCE_LENGTH, KEY_VALUE_HEADS * HEAD_SIZE), jnp.float32), -6.0, 6.0)
    return value_entries.astype(jnp.bfloat16)


def draw_sequence_adapter_list(key, part):

    def one_row(row_key):
        return jax.random.permutation(row_key, TENANT_COUNT)[:PICK].astype(jnp.int32)
    return jax.vmap(one_row)(jax.random.split(jax.random.fold_in(key, 505), PACKED_SEQUENCES))


def place_ends(result, own_key, smallest, largest):
    shape = result.shape
    place = [jax.random.randint(jax.random.fold_in(own_key, axis), (), 0, shape[axis]) for axis in range(len(shape))]
    result = result.at[tuple(place)].set(smallest)
    longest = shape.index(max(shape))
    place[longest] = (place[longest] + 1) % shape[longest]
    return result.at[tuple(place)].set(largest)


def block_levels(own_key, extent, shards, least, top_value):
    loudness = 1.0
    for dim, blocks in shards:
        heights = jax.random.uniform(jax.random.fold_in(jax.random.fold_in(own_key, 6), dim), (blocks,), jnp.float32, least / len(shards), top_value / len(shards))
        loudness = loudness * jnp.repeat(jnp.exp(heights), extent[dim] // blocks).reshape((-1,) + (1,) * (len(extent) - 1 - dim))
    return loudness


def rank_table(count, lean):
    portions = [(1 << 20) // math.isqrt(grade ** lean) + 1 for grade in range(1, count + 1)]
    scale = 1 + sum(portions) // (1 << 30)
    return np.cumsum(np.array([max(1, weight // scale) for weight in portions]))


def ranked_ids(stream_key, shape, amount, skew):
    listing = rank_table(amount, skew)
    ticket = jax.random.randint(jax.random.fold_in(stream_key, 1), shape, 0, int(listing[amount - 1]))
    grade = jnp.searchsorted(jnp.asarray(listing, jnp.int32), ticket, side="right")
    return jax.random.permutation(jax.random.fold_in(stream_key, 2), amount)[grade].astype(jnp.int32)


def centred(stream_key, extent, deviation, reach, shards=(), held_as=jnp.bfloat16):
    level = block_levels(stream_key, extent, shards, -0.22, 0.18) if shards else 1.0
    entries = jax.random.normal(stream_key, extent, jnp.float32) * deviation * level
    return jnp.minimum(jnp.maximum(entries, -reach), reach).astype(held_as)


def setup_inputs(seed: int = 0) -> dict:
    keys = jax.random.split(jax.random.key(seed), 11)
    return {
        "normed_hidden_input": centred(keys[0], (PACKED_SEQUENCES, SEQUENCE_LENGTH, MODEL_WIDTH), 1.0, 6.0, ((0, 16), (1, 16))),
        "frozen_query_base": draw_frozen_query_base(jax.random.fold_in(keys[10], 71), 0),
        "key_head_states": draw_key_head_states(jax.random.fold_in(keys[10], 71), 0),
        "value_head_states": centred(keys[3], (PACKED_SEQUENCES, SEQUENCE_LENGTH, KEY_VALUE_HEADS * HEAD_SIZE), 1.0, 6.0, ((0, 16), (1, 16))),
        "document_numbers": draw_document_numbers(jax.random.fold_in(keys[10], 71), 0),
        "tenant_block_entry": place_ends(ranked_ids(keys[5], (PACKED_SEQUENCES, NBLK), PICK, 2), jax.random.fold_in(keys[5], 3), 0, PICK - 1).astype(jnp.int32),
        "sequence_adapter_list": draw_sequence_adapter_list(jax.random.fold_in(keys[10], 71), 0),
        "adapter_down_weight": centred(keys[7], (TENANT_COUNT, ADAPTER_RANK, MODEL_WIDTH), MODEL_WIDTH ** -0.5, 0.09375, ((0, 16), (2, 16))),
        "adapter_up_weight": centred(keys[8], (TENANT_COUNT, ADAPTER_RANK, QUERY_HEADS * HEAD_SIZE), ADAPTER_RANK ** -0.5, 0.75, ((0, 16), (2, 16))),
        "output_gradient": centred(keys[9], (PACKED_SEQUENCES, SEQUENCE_LENGTH, QUERY_HEADS * HEAD_SIZE), 1.0, 6.0, ((0, 16), (1, 16))),
    }


masked_fill_value = -1e+30

def low_cast(value_entries):
    return lax.optimization_barrier(value_entries.astype(jnp.bfloat16)).astype(jnp.float32)

def reference(normed_hidden_input, frozen_query_base, key_head_states, value_head_states, document_numbers, tenant_block_entry, sequence_adapter_list, adapter_down_weight, adapter_up_weight, output_gradient):
    head_groupings = QUERY_HEADS // KEY_VALUE_HEADS
    score_scale = 1.0 / math.sqrt(HEAD_SIZE)
    query_width = QUERY_HEADS * HEAD_SIZE
    rows_block = math.gcd(SEQUENCE_LENGTH, 512)
    block_total = SEQUENCE_LENGTH // rows_block
    positions = jnp.arange(SEQUENCE_LENGTH, dtype=jnp.int32)
    slot_range = jnp.arange(PICK, dtype=jnp.int32)

    def one_sequence(totals, inputs):
        down_total, up_total = totals
        tokens, base_rows, key_row_block, value_row_block, doc_row, slot_row, selected_tenant, gradient_row_block = inputs
        down_selected = jnp.take(adapter_down_weight, selected_tenant, axis=0)
        up_selected = jnp.take(adapter_up_weight, selected_tenant, axis=0)
        up_flat = up_selected.reshape(PICK * ADAPTER_RANK, query_width)
        token_slot = jnp.repeat(slot_row, TB)
        picker = (token_slot[:, None] == slot_range[None, :])[:, :, None]
        low_each = jnp.einsum('td,krd->tkr', tokens.astype(jnp.float32), down_selected.astype(jnp.float32))
        low_rank = lax.optimization_barrier(jnp.sum(jnp.where(picker, low_each, 0.0), axis=1)).astype(jnp.bfloat16)
        spread_low = jnp.where(picker, low_rank[:, None, :], jnp.zeros((), jnp.bfloat16)).reshape(SEQUENCE_LENGTH, PICK * ADAPTER_RANK)
        lifted = jnp.dot(spread_low, up_flat, preferred_element_type=jnp.float32)
        query_rows = (base_rows.astype(jnp.float32) + lifted).astype(jnp.bfloat16)
        query_head_rows = query_rows.reshape(SEQUENCE_LENGTH, KEY_VALUE_HEADS, head_groupings, HEAD_SIZE).astype(jnp.float32)
        key_head_rows = key_row_block.reshape(SEQUENCE_LENGTH, KEY_VALUE_HEADS, HEAD_SIZE).astype(jnp.float32)
        value_head_rows = value_row_block.reshape(SEQUENCE_LENGTH, KEY_VALUE_HEADS, HEAD_SIZE).astype(jnp.float32)
        gradient_head_rows = gradient_row_block.reshape(SEQUENCE_LENGTH, KEY_VALUE_HEADS, head_groupings, HEAD_SIZE).astype(jnp.float32)

        def block_mask(block_index):
            first_row = block_index * rows_block
            query_pos = first_row + jnp.arange(rows_block, dtype=jnp.int32)
            query_doc = lax.dynamic_slice_in_dim(doc_row, first_row, rows_block, 0)
            allowed = (query_doc[:, None] == doc_row[None, :]) & (positions[None, :] <= query_pos[:, None])
            return (first_row, allowed)

        def forward_rows(block_index):
            first_row, allowed = block_mask(block_index)
            block_queries = lax.dynamic_slice_in_dim(query_head_rows, first_row, rows_block, 0)
            scores = jnp.einsum('tkgd,skd->kgts', block_queries, key_head_rows) * score_scale
            scores = jnp.where(allowed, scores, masked_fill_value)
            row_peak = lax.optimization_barrier(jnp.max(scores, axis=-1))
            weights = jnp.where(allowed, jnp.exp(scores - row_peak[..., None]), 0.0)
            weight_total = lax.optimization_barrier(jnp.sum(weights, axis=-1))
            mixed_sum = jnp.einsum('kgts,skd->kgtd', low_cast(weights), value_head_rows)
            block_out = (mixed_sum / weight_total[..., None]).transpose(2, 0, 1, 3).reshape(rows_block, query_width)
            return (block_out.astype(jnp.bfloat16), row_peak + jnp.log(weight_total))
        out_blocks, log_blocks = lax.map(forward_rows, jnp.arange(block_total, dtype=jnp.int32))
        attention_row_block = out_blocks.reshape(SEQUENCE_LENGTH, query_width)
        output_head_rows = attention_row_block.reshape(SEQUENCE_LENGTH, KEY_VALUE_HEADS, head_groupings, HEAD_SIZE).astype(jnp.float32)
        delta_sum = jnp.einsum('tkgd,tkgd->kgt', gradient_head_rows, output_head_rows)

        def backward_rows(grad_sums, block_index):
            key_gradient_sum, value_gradient_sum = grad_sums
            first_row, allowed = block_mask(block_index)
            block_queries = lax.dynamic_slice_in_dim(query_head_rows, first_row, rows_block, 0)
            block_grads = lax.dynamic_slice_in_dim(gradient_head_rows, first_row, rows_block, 0)
            log_total = log_blocks[block_index]
            block_delta = lax.dynamic_slice_in_dim(delta_sum, first_row, rows_block, 2)
            scores = jnp.einsum('tkgd,skd->kgts', block_queries, key_head_rows) * score_scale
            probabilities = jnp.where(allowed, jnp.exp(jnp.where(allowed, scores, masked_fill_value) - log_total[..., None]), 0.0)
            value_part = jnp.einsum('kgts,tkgd->skd', low_cast(probabilities), block_grads)
            dprobs = jnp.einsum('tkgd,skd->kgts', block_grads, value_head_rows)
            dscores = low_cast(probabilities * (dprobs - block_delta[..., None]))
            query_grad = score_scale * jnp.einsum('kgts,skd->tkgd', dscores, key_head_rows)
            key_part = score_scale * jnp.einsum('kgts,tkgd->skd', dscores, block_queries)
            return ((key_gradient_sum + key_part, value_gradient_sum + value_part), query_grad.reshape(rows_block, query_width))
        zeroed_row_block = jnp.zeros((SEQUENCE_LENGTH, KEY_VALUE_HEADS, HEAD_SIZE), jnp.float32)
        grad_sums, grad_blocks = lax.scan(backward_rows, (zeroed_row_block, zeroed_row_block), jnp.arange(block_total, dtype=jnp.int32))
        key_gradient_sum, value_gradient_sum = grad_sums
        query_grad_low = grad_blocks.reshape(SEQUENCE_LENGTH, query_width).astype(jnp.bfloat16)
        up_part = lax.dot_general(spread_low, query_grad_low, (((0,), (0,)), ((), ())), preferred_element_type=jnp.float32)
        low_grad_each = jnp.dot(query_grad_low, up_flat.T, preferred_element_type=jnp.float32).reshape(SEQUENCE_LENGTH, PICK, ADAPTER_RANK)
        low_grad = lax.optimization_barrier(jnp.sum(jnp.where(picker, low_grad_each, 0.0), axis=1)).astype(jnp.bfloat16)
        spread_grad = jnp.where(picker, low_grad[:, None, :], jnp.zeros((), jnp.bfloat16)).reshape(SEQUENCE_LENGTH, PICK * ADAPTER_RANK)
        down_part = lax.dot_general(spread_grad, tokens, (((0,), (0,)), ((), ())), preferred_element_type=jnp.float32)
        down_total = down_total.at[selected_tenant].add(down_part.reshape(PICK, ADAPTER_RANK, MODEL_WIDTH))
        up_total = up_total.at[selected_tenant].add(up_part.reshape(PICK, ADAPTER_RANK, query_width))
        attention_results = (attention_row_block, key_gradient_sum.reshape(SEQUENCE_LENGTH, KEY_VALUE_HEADS * HEAD_SIZE), value_gradient_sum.reshape(SEQUENCE_LENGTH, KEY_VALUE_HEADS * HEAD_SIZE))
        return ((down_total, up_total), attention_results)
    zero_down = jnp.zeros((TENANT_COUNT, ADAPTER_RANK, MODEL_WIDTH), jnp.float32)
    zero_up = jnp.zeros((TENANT_COUNT, ADAPTER_RANK, QUERY_HEADS * HEAD_SIZE), jnp.float32)
    inputs = (normed_hidden_input, frozen_query_base, key_head_states, value_head_states, document_numbers, tenant_block_entry, sequence_adapter_list, output_gradient)
    totals, attention_results = lax.scan(one_sequence, (zero_down, zero_up), inputs)
    down_grad, up_grad = totals
    attention_out, key_grad, value_grad = attention_results
    return (attention_out, key_grad, value_grad, down_grad, up_grad)
```

```python
import functools
import math

import jax
import jax.numpy as jnp
from jax import lax
from jax.experimental import pallas as pl
from jax.experimental.pallas import tpu as pltpu
from jax.sharding import PartitionSpec as P

MESH = pl.DeviceIdType.MESH
BF16 = jnp.bfloat16
F32 = jnp.float32
HEAD = 128
RANK = 64
TB = 32
QUERY_BLOCK = 256
KEY_BLOCK = 512
MASKED = -1e30
SCALE = 1.0 / math.sqrt(HEAD)
LOG2E = math.log2(math.e)


def dot(a, b):
    return lax.dot_general(a, b, (((1,), (0,)), ((), ())), preferred_element_type=F32)


def dot_nt(a, b):
    return lax.dot_general(a, b, (((1,), (1,)), ((), ())), preferred_element_type=F32)


def aligned(index, size):
    return pl.ds(pl.multiple_of(index * size, size), size)


class Exchange:
    def __init__(self, axis, count, me, source, target, send, recv, local):
        self.axis, self.count, self.me = axis, count, me
        self.source, self.target = source, target
        self.send, self.recv, self.local = send, recv, local

    def copy(self, peer, place):
        return pltpu.make_async_remote_copy(
            src_ref=self.source(peer),
            dst_ref=self.target(place),
            send_sem=self.send.at[peer],
            recv_sem=self.recv.at[place],
            device_id={self.axis: peer},
            device_id_type=MESH,
        )

    def own(self):
        return pltpu.make_async_copy(self.source(self.me), self.target(self.me), self.local)

    def each(self, body):
        def step(shift, carry):
            body(lax.rem(self.me + shift, self.count))
            return carry

        lax.fori_loop(1, self.count, step, 0)

    def start(self):
        self.each(lambda peer: self.copy(peer, self.me).start())
        if self.local is not None:
            self.own().start()

    def wait_recv(self):
        self.each(lambda peer: self.copy(peer, peer).wait_recv())
        if self.local is not None:
            self.own().wait()

    def wait_send(self):
        self.each(lambda peer: self.copy(peer, self.me).wait_send())


def meet(me_ctx, ctx_count, me_seq, seq_count):
    barrier = pltpu.get_barrier_semaphore()

    def greet(axis, me, count):
        def step(shift, carry):
            pl.semaphore_signal(
                barrier,
                inc=1,
                device_id={axis: lax.rem(me + shift, count)},
                device_id_type=MESH,
            )
            return carry

        lax.fori_loop(1, count, step, 0)

    greet("ctx", me_ctx, ctx_count)
    greet("seq", me_seq, seq_count)
    pl.semaphore_wait(barrier, ctx_count + seq_count - 2)


def spread_slots(slot_row, low, picks):
    zero = jnp.zeros_like(low)
    return jnp.concatenate(
        [jnp.where(slot_row == pick, low, zero) for pick in range(picks)], axis=0
    )


def fold_slots(slot_row, each, picks):
    total = jnp.zeros((RANK, each.shape[1]), F32)
    for pick in range(picks):
        part = each[pick * RANK : (pick + 1) * RANK]
        total = total + jnp.where(slot_row == pick, part, 0.0)
    return total


def gather_kernel(
    ctx_count,
    seq_count,
    group,
    tokens,
    base,
    key,
    value,
    gradient,
    meta,
    down,
    up,
    adapters,
    tokens_all,
    base_all,
    key_all,
    value_all,
    gradient_all,
    meta_all,
    low_all,
    up_picked,
    down_tenants,
    up_tenants,
    down_picked,
    low_part,
    low_recv,
    send,
    recv,
    send_seq,
    recv_seq,
    local,
):
    me = lax.axis_index("ctx")
    own_seq = lax.axis_index("seq")
    rows = tokens.shape[0]
    width = tokens_all.shape[1]
    picks = adapters.shape[1]

    def over_ctx(slot, source, target, has_own=True):
        return Exchange(
            "ctx",
            ctx_count,
            me,
            source,
            target,
            send.at[slot],
            recv.at[slot],
            local.at[slot] if has_own else None,
        )

    def over_seq(slot, source, target):
        return Exchange(
            "seq",
            seq_count,
            own_seq,
            source,
            target,
            send_seq.at[slot],
            recv_seq.at[slot],
            local.at[8 + slot],
        )

    x_move = over_ctx(
        0,
        lambda peer: tokens.at[:, aligned(peer, width)],
        lambda place: tokens_all.at[aligned(place, rows), :],
    )
    meta_move = over_ctx(
        1, lambda peer: meta, lambda place: meta_all.at[:, aligned(place, rows)]
    )
    key_move = over_ctx(
        2,
        lambda peer: key.at[:, aligned(peer // group, HEAD)],
        lambda place: key_all.at[aligned(place, rows), :],
    )
    base_move = over_ctx(
        3,
        lambda peer: base.at[:, aligned(peer, HEAD)],
        lambda place: base_all.at[aligned(place, rows), :],
    )
    value_move = over_ctx(
        4,
        lambda peer: value.at[:, aligned(peer // group, HEAD)],
        lambda place: value_all.at[aligned(place, rows), :],
    )
    gradient_move = over_ctx(
        5,
        lambda peer: gradient.at[:, aligned(peer, HEAD)],
        lambda place: gradient_all.at[aligned(place, rows), :],
    )
    partial_move = over_ctx(
        6,
        lambda peer: low_part.at[:, aligned(peer, rows)],
        lambda place: low_recv.at[place],
    )
    low_move = over_ctx(
        7,
        lambda peer: low_all.at[:, aligned(me, rows)],
        lambda place: low_all.at[:, aligned(place, rows)],
        has_own=False,
    )
    down_move = over_seq(0, lambda peer: down, lambda place: down_tenants.at[place])
    up_move = over_seq(1, lambda peer: up, lambda place: up_tenants.at[place])

    meet(me, ctx_count, own_seq, seq_count)
    down_move.start()
    x_move.start()
    meta_move.start()
    up_move.start()
    key_move.start()
    base_move.start()
    value_move.start()
    gradient_move.start()

    meta_move.wait_recv()
    down_move.wait_recv()
    for pick in range(picks):
        down_picked[pick * RANK : (pick + 1) * RANK, :] = down_tenants[adapters[own_seq, pick]]
    x_move.wait_recv()
    chunk = 2 * rows

    def low_step(step, carry):
        place = aligned(step, chunk)
        each = dot_nt(down_picked[...], tokens_all[place, :])
        low_part[:, place] = fold_slots(meta_all[1:2, place], each, picks).astype(BF16)
        return carry

    lax.fori_loop(0, ctx_count // 2, low_step, 0)
    partial_move.start()
    up_move.wait_recv()
    for pick in range(picks):
        up_picked[pick * RANK : (pick + 1) * RANK, :] = up_tenants[adapters[own_seq, pick]]
    partial_move.wait_recv()

    def add_step(step, total):
        return total + low_recv[step].astype(F32)

    low_own = lax.fori_loop(0, ctx_count, add_step, jnp.zeros((RANK, rows), F32))
    low_all[:, aligned(me, rows)] = low_own.astype(BF16)
    low_move.start()
    key_move.wait_recv()
    base_move.wait_recv()
    value_move.wait_recv()
    gradient_move.wait_recv()
    low_move.wait_recv()
    for move in (
        x_move,
        meta_move,
        key_move,
        base_move,
        value_move,
        gradient_move,
        partial_move,
        low_move,
        down_move,
        up_move,
    ):
        move.wait_send()


def attention_kernel(
    base,
    key,
    value,
    gradient,
    meta,
    low,
    up_picked,
    adapters,
    out,
    key_grad,
    value_grad,
    low_grad,
    up_table,
    key_t,
    value_t,
    up_t,
    scores,
    weights,
    key_sum,
    value_sum,
    up_sum,
):
    length = base.shape[0]
    picks = adapters.shape[1]
    own_seq = lax.axis_index("seq")
    query_block = min(QUERY_BLOCK, length)
    key_block = min(KEY_BLOCK, length)
    key_t[...] = jnp.transpose(key[...])
    value_t[...] = jnp.transpose(value[...])
    up_t[...] = jnp.transpose(up_picked[...])
    key_sum[...] = jnp.zeros_like(key_sum)
    value_sum[...] = jnp.zeros_like(value_sum)
    up_sum[...] = jnp.zeros_like(up_sum)
    documents = meta[0:1, :]
    cuts = [
        jnp.sum(jnp.where(documents < number, 1.0, 0.0)).astype(jnp.int32) for number in (1, 2, 3)
    ]

    def query_step(step, carry):
        first = step * query_block
        place = aligned(step, query_block)
        slot_row = meta[1:2, place]
        low_spread = spread_slots(slot_row, low[:, place], picks)
        lifted = dot(up_t[...], low_spread)
        queries = (base[place, :].astype(F32) + jnp.transpose(lifted)).astype(BF16)
        position = first + lax.broadcasted_iota(jnp.int32, (1, query_block), 1)
        start = jnp.zeros((1, query_block), jnp.int32)
        first_start = jnp.int32(0)
        for cut in cuts:
            start = jnp.where(position >= cut, cut, start)
            first_start = jnp.where(first >= cut, cut, first_start)
        low_block = first_start // key_block
        high_block = (first + query_block - 1) // key_block + 1

        def score_step(block, peak):
            keys = aligned(block, key_block)
            logits = dot_nt(key[keys, :], queries) * (SCALE * LOG2E)
            key_position = block * key_block + lax.broadcasted_iota(
                jnp.int32, (key_block, query_block), 0
            )
            logits = jnp.where(
                (key_position <= position) & (key_position >= start), logits, MASKED
            )
            scores[keys, :] = logits
            return jnp.maximum(peak, jnp.max(logits.reshape(-1, 8, query_block), axis=0))

        peak8 = lax.fori_loop(
            low_block, high_block, score_step, jnp.full((8, query_block), MASKED, F32)
        )
        peak = jnp.max(peak8, axis=0, keepdims=True)

        def weight_step(block, state):
            total, mixed = state
            keys = aligned(block, key_block)
            weight = jnp.exp2(scores[keys, :] - peak)
            weight_low = weight.astype(BF16)
            weights[keys, :] = weight_low
            total = total + jnp.sum(weight.reshape(-1, 8, query_block), axis=0)
            return total, mixed + dot(value_t[:, keys], weight_low)

        total8, mixed = lax.fori_loop(
            low_block,
            high_block,
            weight_step,
            (jnp.zeros((8, query_block), F32), jnp.zeros((HEAD, query_block), F32)),
        )
        inverse = 1.0 / jnp.sum(total8, axis=0, keepdims=True)
        mixed_low = (mixed * inverse).astype(BF16)
        out[place, :] = jnp.transpose(mixed_low)
        gradient_t = jnp.transpose(gradient[place, :]).astype(F32) * inverse
        delta = jnp.sum(gradient_t * mixed_low.astype(F32), axis=0, keepdims=True)
        gradient_low = jnp.transpose(gradient_t.astype(BF16))

        def back_step(block, query_sum):
            keys = aligned(block, key_block)
            weight_low = weights[keys, :]
            value_sum[keys, :] += dot(weight_low, gradient_low)
            dprobs = dot_nt(value[keys, :], gradient_low)
            dscores = (weight_low.astype(F32) * (dprobs - delta)).astype(BF16)
            key_sum[keys, :] += dot(dscores, queries)
            return query_sum + dot(key_t[:, keys], dscores)

        query_sum = lax.fori_loop(
            low_block, high_block, back_step, jnp.zeros((HEAD, query_block), F32)
        )
        query_grad = (query_sum * SCALE).astype(BF16)
        each = dot(up_picked[...], query_grad)
        low_grad[:, place] = fold_slots(slot_row, each, picks).astype(BF16)
        up_sum[...] += dot_nt(low_spread, query_grad)
        return carry

    lax.fori_loop(0, length // query_block, query_step, 0)
    key_grad[...] = (key_sum[...] * SCALE).astype(BF16)
    value_grad[...] = value_sum[...].astype(BF16)
    up_table[...] = jnp.zeros_like(up_table)
    for pick in range(picks):
        up_table[adapters[own_seq, pick]] = up_sum[pick * RANK : (pick + 1) * RANK, :].astype(BF16)


def reduce_kernel(
    ctx_count,
    seq_count,
    group,
    out,
    key_part,
    value_part,
    low_part,
    tokens_all,
    meta,
    up_table,
    adapters,
    attention,
    key_grad,
    value_grad,
    down_grad,
    up_grad,
    key_recv,
    value_recv,
    low_recv,
    low_all,
    down_sum,
    down_table,
    down_recv,
    up_recv,
    send,
    recv,
    send_seq,
    recv_seq,
    local,
):
    me = lax.axis_index("ctx")
    own_seq = lax.axis_index("seq")
    rows = attention.shape[0]
    length = tokens_all.shape[0]
    picks = adapters.shape[1]

    def over_ctx(slot, source, target, has_own=True):
        return Exchange(
            "ctx",
            ctx_count,
            me,
            source,
            target,
            send.at[slot],
            recv.at[slot],
            local.at[slot] if has_own else None,
        )

    def over_seq(slot, source, target):
        return Exchange(
            "seq",
            seq_count,
            own_seq,
            source,
            target,
            send_seq.at[slot],
            recv_seq.at[slot],
            local.at[5 + slot],
        )

    partial_move = over_ctx(
        0,
        lambda peer: low_part.at[:, aligned(peer, rows)],
        lambda place: low_recv.at[place],
    )
    low_move = over_ctx(
        1,
        lambda peer: low_all.at[:, aligned(me, rows)],
        lambda place: low_all.at[:, aligned(place, rows)],
        has_own=False,
    )
    out_move = over_ctx(
        2,
        lambda peer: out.at[aligned(peer, rows), :],
        lambda place: attention.at[:, aligned(place, HEAD)],
    )
    key_move = over_ctx(
        3, lambda peer: key_part.at[aligned(peer, rows), :], lambda place: key_recv.at[place]
    )
    value_move = over_ctx(
        4, lambda peer: value_part.at[aligned(peer, rows), :], lambda place: value_recv.at[place]
    )
    up_move = over_seq(0, lambda peer: up_table.at[peer], lambda place: up_recv.at[place])
    down_move = over_seq(1, lambda peer: down_table.at[peer], lambda place: down_recv.at[place])

    meet(me, ctx_count, own_seq, seq_count)
    partial_move.start()
    out_move.start()
    up_move.start()
    partial_move.wait_recv()

    def add_step(step, total):
        return total + low_recv[step].astype(F32)

    low_own = lax.fori_loop(0, ctx_count, add_step, jnp.zeros((RANK, rows), F32))
    low_all[:, aligned(me, rows)] = low_own.astype(BF16)
    low_move.start()
    key_move.start()
    value_move.start()
    low_move.wait_recv()

    down_sum[...] = jnp.zeros_like(down_sum)
    chunk = 2 * rows

    def down_step(step, carry):
        place = aligned(step, chunk)
        spread = spread_slots(meta[1:2, place], low_all[:, place], picks)
        down_sum[...] += dot(spread, tokens_all[place, :])
        return carry

    lax.fori_loop(0, length // chunk, down_step, 0)
    tenants = [adapters[own_seq, pick] for pick in range(picks)]

    def table_step(tenant, carry):
        total = jnp.zeros(down_grad.shape, F32)
        for pick in range(picks):
            here = (tenants[pick] == tenant).astype(F32)
            total = total + down_sum[pick * RANK : (pick + 1) * RANK, :] * here
        down_table[tenant] = total.astype(BF16)
        return carry

    lax.fori_loop(0, seq_count, table_step, 0)
    down_move.start()
    key_move.wait_recv()
    value_move.wait_recv()
    for head in range(key_grad.shape[1] // HEAD):
        place = slice(head * HEAD, (head + 1) * HEAD)
        for recv_ref, grad in ((key_recv, key_grad), (value_recv, value_grad)):
            total = recv_ref[head * group].astype(F32)
            for member in range(1, group):
                total = total + recv_ref[head * group + member].astype(F32)
            grad[:, place] = total
    out_move.wait_recv()
    up_move.wait_recv()
    up_grad[...] = jnp.zeros_like(up_grad)

    def up_step(step, carry):
        up_grad[...] += up_recv[step].astype(F32)
        return carry

    lax.fori_loop(0, seq_count, up_step, 0)
    down_move.wait_recv()
    down_grad[...] = jnp.zeros_like(down_grad)

    def owner_step(step, carry):
        down_grad[...] += down_recv[step].astype(F32)
        return carry

    lax.fori_loop(0, seq_count, owner_step, 0)
    for move in (partial_move, low_move, out_move, key_move, value_move, up_move, down_move):
        move.wait_send()


def vmem():
    return pl.BlockSpec(memory_space=pltpu.VMEM)


def hbm():
    return pl.BlockSpec(memory_space=pl.ANY)


def smem():
    return pl.BlockSpec(memory_space=pltpu.SMEM)


def per_device(
    normed_hidden_input,
    frozen_query_base,
    key_head_states,
    value_head_states,
    document_numbers,
    tenant_block_entry,
    sequence_adapter_list,
    adapter_down_weight,
    adapter_up_weight,
    output_gradient,
):
    ctx_count = lax.axis_size("ctx")
    seq_count = lax.axis_size("seq")
    rows = normed_hidden_input.shape[1]
    length = rows * ctx_count
    width = adapter_down_weight.shape[2]
    picks = sequence_adapter_list.shape[1]
    key_heads = key_head_states.shape[2] // HEAD
    group = ctx_count // key_heads
    stacked = picks * RANK
    token_slots = jnp.repeat(tenant_block_entry, TB, axis=1)
    meta = jnp.pad(jnp.concatenate([document_numbers, token_slots], axis=0), ((0, 6), (0, 0)))

    def shape(dims, dtype=BF16):
        return jax.ShapeDtypeStruct(dims, dtype)

    gathered = pl.pallas_call(
        functools.partial(gather_kernel, ctx_count, seq_count, group),
        name="gather_heads",
        out_shape=(
            shape((length, width)),
            shape((length, HEAD)),
            shape((length, HEAD)),
            shape((length, HEAD)),
            shape((length, HEAD)),
            shape((8, length), jnp.int32),
            shape((RANK, length)),
            shape((stacked, HEAD)),
        ),
        in_specs=[hbm()] * 8 + [smem()],
        out_specs=(vmem(), hbm(), hbm(), hbm(), hbm(), vmem(), vmem(), vmem()),
        scratch_shapes=[
            pltpu.VMEM((seq_count, RANK, width), BF16),
            pltpu.VMEM((seq_count, RANK, HEAD), BF16),
            pltpu.VMEM((stacked, width), BF16),
            pltpu.VMEM((RANK, length), BF16),
            pltpu.VMEM((ctx_count, RANK, rows), BF16),
            pltpu.SemaphoreType.DMA((8, ctx_count)),
            pltpu.SemaphoreType.DMA((8, ctx_count)),
            pltpu.SemaphoreType.DMA((2, seq_count)),
            pltpu.SemaphoreType.DMA((2, seq_count)),
            pltpu.SemaphoreType.DMA((10,)),
        ],
        compiler_params=pltpu.CompilerParams(
            collective_id=0, has_side_effects=True, vmem_limit_bytes=40 << 20
        ),
    )(
        normed_hidden_input[0],
        frozen_query_base[0],
        key_head_states[0],
        value_head_states[0],
        output_gradient[0],
        meta,
        adapter_down_weight[0],
        adapter_up_weight[0],
        sequence_adapter_list,
    )
    tokens_all, base_all, key_all, value_all, gradient_all, meta_all, low_all, up_picked = gathered

    query_block = min(QUERY_BLOCK, length)
    attended = pl.pallas_call(
        attention_kernel,
        name="attention_one_head",
        out_shape=(
            shape((length, HEAD)),
            shape((length, HEAD)),
            shape((length, HEAD)),
            shape((RANK, length)),
            shape((seq_count, RANK, HEAD)),
        ),
        in_specs=[vmem()] * 7 + [smem()],
        out_specs=(vmem(),) * 5,
        scratch_shapes=[
            pltpu.VMEM((HEAD, length), BF16),
            pltpu.VMEM((HEAD, length), BF16),
            pltpu.VMEM((HEAD, stacked), BF16),
            pltpu.VMEM((length, query_block), F32),
            pltpu.VMEM((length, query_block), BF16),
            pltpu.VMEM((length, HEAD), F32),
            pltpu.VMEM((length, HEAD), F32),
            pltpu.VMEM((stacked, HEAD), F32),
        ],
        compiler_params=pltpu.CompilerParams(vmem_limit_bytes=40 << 20),
    )(
        base_all,
        key_all,
        value_all,
        gradient_all,
        meta_all,
        low_all,
        up_picked,
        sequence_adapter_list,
    )
    out, key_part, value_part, low_part, up_table = attended

    attention, key_grad, value_grad, down_grad, up_grad = pl.pallas_call(
        functools.partial(reduce_kernel, ctx_count, seq_count, group),
        name="return_and_reduce",
        out_shape=(
            shape((rows, ctx_count * HEAD)),
            shape((rows, key_heads * HEAD), F32),
            shape((rows, key_heads * HEAD), F32),
            shape((RANK, width), F32),
            shape((RANK, HEAD), F32),
        ),
        in_specs=[hbm()] * 4 + [vmem(), vmem(), hbm(), smem()],
        out_specs=(hbm(), vmem(), vmem(), vmem(), vmem()),
        scratch_shapes=[
            pltpu.VMEM((ctx_count, rows, HEAD), BF16),
            pltpu.VMEM((ctx_count, rows, HEAD), BF16),
            pltpu.VMEM((ctx_count, RANK, rows), BF16),
            pltpu.VMEM((RANK, length), BF16),
            pltpu.VMEM((stacked, width), F32),
            pltpu.VMEM((seq_count, RANK, width), BF16),
            pltpu.VMEM((seq_count, RANK, width), BF16),
            pltpu.VMEM((seq_count, RANK, HEAD), BF16),
            pltpu.SemaphoreType.DMA((5, ctx_count)),
            pltpu.SemaphoreType.DMA((5, ctx_count)),
            pltpu.SemaphoreType.DMA((2, seq_count)),
            pltpu.SemaphoreType.DMA((2, seq_count)),
            pltpu.SemaphoreType.DMA((7,)),
        ],
        compiler_params=pltpu.CompilerParams(
            collective_id=1, has_side_effects=True, vmem_limit_bytes=40 << 20
        ),
    )(out, key_part, value_part, low_part, tokens_all, meta_all, up_table, sequence_adapter_list)
    return (
        attention[None],
        key_grad[None],
        value_grad[None],
        down_grad[None],
        up_grad[None],
    )


def solution(mesh):
    in_specs = (
        P("seq", "ctx", None),
        P("seq", "ctx", None),
        P("seq", "ctx", None),
        P("seq", "ctx", None),
        P("seq", "ctx"),
        P("seq", "ctx"),
        P(),
        P("seq", None, "ctx"),
        P("seq", None, "ctx"),
        P("seq", "ctx", None),
    )
    out_specs = (
        P("seq", "ctx", None),
        P("seq", "ctx", None),
        P("seq", "ctx", None),
        P("seq", None, "ctx"),
        P("seq", None, "ctx"),
    )
    return jax.shard_map(
        per_device, mesh=mesh, in_specs=in_specs, out_specs=out_specs, check_vma=False
    )
```

```python
import functools
import math

import jax
import jax.numpy as jnp
from jax import lax
from jax.experimental import pallas as pl
from jax.experimental.pallas import tpu as pltpu
from jax.sharding import PartitionSpec as P

MESH = pl.DeviceIdType.MESH
BF16 = jnp.bfloat16
F32 = jnp.float32
HEAD = 128
RANK = 64
TB = 32
KEY_BLOCK = 512
MASKED = -1e30
SCALE = 1.0 / math.sqrt(HEAD)
LOG2E = math.log2(math.e)


def dot(a, b):
    return lax.dot_general(a, b, (((1,), (0,)), ((), ())), preferred_element_type=F32)


def dot_nt(a, b):
    return lax.dot_general(a, b, (((1,), (1,)), ((), ())), preferred_element_type=F32)


def aligned(index, size):
    return pl.ds(pl.multiple_of(index * size, size), size)


def push(source, target, send, recv, dest):
    return pltpu.make_async_remote_copy(
        src_ref=source,
        dst_ref=target,
        send_sem=send,
        recv_sem=recv,
        device_id=dest,
        device_id_type=MESH,
    )


def loop(low, high, body):
    def step(index, carry):
        body(index)
        return carry

    lax.fori_loop(low, high, step, 0)


class Exchange:
    def __init__(self, axis, count, me, source, target, send, recv, local):
        self.axis, self.count, self.me = axis, count, me
        self.source, self.target = source, target
        self.send, self.recv, self.local = send, recv, local

    def copy(self, peer, place):
        return push(
            self.source(peer),
            self.target(place),
            self.send.at[peer],
            self.recv.at[place],
            {self.axis: peer},
        )

    def own(self):
        return pltpu.make_async_copy(self.source(self.me), self.target(self.me), self.local)

    def each(self, body):
        loop(1, self.count, lambda shift: body(lax.rem(self.me + shift, self.count)))

    def start(self):
        self.each(lambda peer: self.copy(peer, self.me).start())
        self.own().start()

    def wait_from(self, place):
        self.copy(place, place).wait_recv()

    def wait_recv(self):
        self.each(self.wait_from)
        self.own().wait()

    def wait_send(self):
        self.each(lambda peer: self.copy(peer, self.me).wait_send())


class Column:
    def __init__(self, planes, plane, side, send, recv):
        self.planes, self.plane, self.side = planes, plane, side
        self.send, self.recv = send, recv

    def to_plane(self, source, target, there):
        dest = {"ctx": there * 2 + self.side}
        push(source, target, self.send.at[there], self.recv.at[self.plane], dest).start()

    def to_twin(self, source, target, index):
        dest = {"ctx": self.plane * 2 + 1 - self.side}
        push(source, target, self.send.at[index], self.recv.at[index], dest).start()

    def got(self, target, index):
        dest = {"ctx": self.plane * 2 + 1 - self.side}
        push(target, target, self.send.at[index], self.recv.at[index], dest).wait_recv()

    def sent(self, source, index):
        dest = {"ctx": self.plane * 2 + 1 - self.side}
        push(source, source, self.send.at[index], self.recv.at[index], dest).wait_send()

    def others(self, body):
        loop(1, self.planes, lambda shift: body(lax.rem(self.plane + shift, self.planes)))

    def every(self, body):
        loop(0, self.planes, lambda shift: body(lax.rem(self.plane + shift, self.planes)))


def meet(me_ctx, ctx_count, me_seq, seq_count):
    barrier = pltpu.get_barrier_semaphore()

    def greet(axis, me, count):
        def step(shift):
            pl.semaphore_signal(
                barrier,
                inc=1,
                device_id={axis: lax.rem(me + shift, count)},
                device_id_type=MESH,
            )

        loop(1, count, step)

    greet("ctx", me_ctx, ctx_count)
    greet("seq", me_seq, seq_count)
    pl.semaphore_wait(barrier, ctx_count + seq_count - 2)


def spread_slots(slot_row, low, picks):
    zero = jnp.zeros_like(low)
    return jnp.concatenate(
        [jnp.where(slot_row == pick, low, zero) for pick in range(picks)], axis=0
    )


def fold_slots(slot_row, each, picks):
    total = jnp.zeros((RANK, each.shape[1]), F32)
    for pick in range(picks):
        part = each[pick * RANK : (pick + 1) * RANK]
        total = total + jnp.where(slot_row == pick, part, 0.0)
    return total


def fused_kernel(
    ctx_count,
    seq_count,
    group,
    tokens,
    base,
    key,
    value,
    gradient,
    meta,
    down,
    up,
    adapters,
    attention,
    key_grad,
    value_grad,
    down_grad,
    up_grad,
    tokens_all,
    base_all,
    key_all,
    value_all,
    gradient_all,
    meta_all,
    down_tenants,
    up_tenants,
    down_picked,
    up_picked,
    up_t,
    low_part,
    low_pair,
    low_sum,
    low_recv,
    low_all,
    grad_part,
    grad_pair,
    grad_sum,
    grad_recv,
    grad_all,
    queries_all,
    out_all,
    weights,
    scores,
    stats,
    key_t,
    value_t,
    key_sum,
    value_sum,
    key_out,
    key_pair,
    key_mid,
    key_recv,
    value_out,
    value_pair,
    value_mid,
    value_recv,
    up_sum,
    up_table,
    up_recv,
    down_sum,
    down_table,
    down_recv,
    send,
    recv,
    send_z,
    recv_z,
    send_seq,
    recv_seq,
    local,
):
    me = lax.axis_index("ctx")
    own_seq = lax.axis_index("seq")
    planes = ctx_count // 2
    plane, side = me // 2, lax.rem(me, 2)
    other = 1 - side
    rows = tokens.shape[0]
    block = 2 * rows
    length = tokens_all.shape[0]
    width = tokens_all.shape[1]
    picks = adapters.shape[1]
    key_block = min(KEY_BLOCK, length)

    def over_ctx(slot, source, target):
        return Exchange(
            "ctx", ctx_count, me, source, target, send.at[slot], recv.at[slot], local.at[slot]
        )

    def over_seq(slot, source, target):
        return Exchange(
            "seq",
            seq_count,
            own_seq,
            source,
            target,
            send_seq.at[slot],
            recv_seq.at[slot],
            local.at[5 + slot],
        )

    columns = [
        Column(planes, plane, side, send_z.at[slot], recv_z.at[slot])
        for slot in range(send_z.shape[0])
    ]
    x_move = over_ctx(
        0,
        lambda peer: tokens.at[:, aligned(peer, width)],
        lambda place: tokens_all.at[aligned(place, rows), :],
    )
    meta_move = over_ctx(
        1, lambda peer: meta, lambda place: meta_all.at[:, aligned(place, rows)]
    )
    base_move = over_ctx(
        2,
        lambda peer: base.at[:, aligned(peer, HEAD)],
        lambda place: base_all.at[aligned(place, rows), :],
    )
    gradient_move = over_ctx(
        3,
        lambda peer: gradient.at[:, aligned(peer, HEAD)],
        lambda place: gradient_all.at[aligned(place, rows), :],
    )
    out_move = over_ctx(
        4,
        lambda peer: out_all.at[aligned(peer, rows), :],
        lambda place: attention.at[:, aligned(place, HEAD)],
    )
    down_move = over_seq(0, lambda peer: down, lambda place: down_tenants.at[place])
    up_move = over_seq(1, lambda peer: up, lambda place: up_tenants.at[place])
    up_back = over_seq(2, lambda peer: up_table.at[peer], lambda place: up_recv.at[place])
    down_back = over_seq(3, lambda peer: down_table.at[peer], lambda place: down_recv.at[place])
    both = (
        (key, key_all, columns[0], columns[1], local.at[9]),
        (value, value_all, columns[2], columns[3], local.at[10]),
    )

    meet(me, ctx_count, own_seq, seq_count)
    down_move.start()
    meta_move.start()
    x_move.start()
    up_move.start()

    def head_of(there):
        return aligned((2 * there) // group, HEAD)

    def own_rows():
        return aligned(me, rows)

    for source, target, column, _, own_sem in both:
        column.others(
            lambda there, source=source, target=target, column=column: column.to_plane(
                source.at[:, head_of(there)], target.at[own_rows(), :], there
            )
        )
        pltpu.make_async_copy(
            source.at[:, head_of(plane)], target.at[own_rows(), :], own_sem
        ).start()
    base_move.start()

    meta_move.wait_recv()
    down_move.wait_recv()
    for pick in range(picks):
        down_picked[pick * RANK : (pick + 1) * RANK, :] = down_tenants[adapters[own_seq, pick]]

    low_pair_column, low_column, low_gather, low_share = columns[4:8]
    x_move.own().wait()

    def low_step(there):
        for part in range(2):
            place = 2 * there + part

            @pl.when(place != me)
            def _():
                x_move.wait_from(place)

        cols = aligned(there, block)
        each = dot_nt(down_picked[...], tokens_all[cols, :])
        low = fold_slots(meta_all[1:2, cols], each, picks).astype(BF16)
        low_part[there, 0] = low[:, :rows]
        low_part[there, 1] = low[:, rows:]
        low_pair_column.to_twin(low_part.at[there, other], low_pair.at[there], there)

    columns[4].every(low_step)

    def reduce_column(pair_column, column, part, pair, total, recv_ref):
        def pair_step(there):
            pair_column.got(pair.at[there], there)
            total[there] = (
                part[there, side].astype(F32) + pair[there].astype(F32)
            ).astype(BF16)

            @pl.when(there != plane)
            def _():
                column.to_plane(total.at[there], recv_ref.at[plane], there)

        column.every(pair_step)

    def finish_column(column, total, recv_ref):
        recv_ref[plane] = total[plane]
        column.others(lambda there: column.got(recv_ref.at[there], there))
        return lax.fori_loop(
            0,
            planes,
            lambda there, acc: acc + recv_ref[there].astype(F32),
            jnp.zeros((RANK, rows), F32),
        ).astype(BF16)

    def gather_start(column, share, all_ref):
        column.others(lambda there: column.to_plane(all_ref.at[me], all_ref.at[me], there))
        share.to_twin(all_ref.at[me], all_ref.at[me], plane)

    def gather_finish(column, share, all_ref):
        def forward(there):
            place = 2 * there + side
            column.got(all_ref.at[place], there)
            share.to_twin(all_ref.at[place], all_ref.at[place], there)

        column.others(forward)
        share.every(lambda there: share.got(all_ref.at[2 * there + other], there))

    reduce_column(low_pair_column, low_column, low_part, low_pair, low_sum, low_recv)
    gradient_move.start()
    low_all[me] = finish_column(low_column, low_sum, low_recv)
    gather_start(low_gather, low_share, low_all)

    for source, target, column, share, own_sem in both:
        pltpu.make_async_copy(
            source.at[:, head_of(plane)], target.at[own_rows(), :], own_sem
        ).wait()

        def forward(there, target=target, column=column, share=share):
            place = target.at[aligned(2 * there + side, rows), :]

            @pl.when(there != plane)
            def _():
                column.got(place, there)

            share.to_twin(place, place, there)

        column.every(forward)
    gather_finish(low_gather, low_share, low_all)
    up_move.wait_recv()
    for pick in range(picks):
        up_picked[pick * RANK : (pick + 1) * RANK, :] = up_tenants[adapters[own_seq, pick]]
    up_t[...] = jnp.transpose(up_picked[...])
    for source, target, column, share, own_sem in both:
        share.every(
            lambda there, target=target, share=share: share.got(
                target.at[aligned(2 * there + other, rows), :], there
            )
        )
    key_t[...] = jnp.transpose(key_all[...])
    value_t[...] = jnp.transpose(value_all[...])
    base_move.wait_recv()

    documents = meta_all[0:1, :]
    cuts = [
        jnp.sum(jnp.where(documents < number, 1, 0), axis=1, keepdims=True) for number in (1, 2, 3)
    ]

    def slots_of(there, all_ref):
        slot_row = meta_all[1:2, aligned(there, block)]
        low = jnp.concatenate([all_ref[2 * there], all_ref[2 * there + 1]], axis=1)
        return slot_row, spread_slots(slot_row, low, picks)

    def blocks_of(there):
        return (there * block + block - 1) // key_block + 1

    def forward_step(there):
        place = aligned(there, block)
        _, low_spread = slots_of(there, low_all)
        lifted = dot(up_t[...], low_spread)
        queries = (base_all[place, :].astype(F32) + jnp.transpose(lifted)).astype(BF16)
        queries_all[place, :] = queries
        position = there * block + lax.broadcasted_iota(jnp.int32, (1, block), 1)
        start = jnp.zeros((1, block), jnp.int32)
        for cut in cuts:
            start = jnp.where(position >= cut, cut, start)

        def score_step(index, peak):
            keys = aligned(index, key_block)
            logits = dot_nt(key_all[keys, :], queries) * (SCALE * LOG2E)
            key_position = index * key_block + lax.broadcasted_iota(
                jnp.int32, (key_block, block), 0
            )
            logits = jnp.where(
                (key_position <= position) & (key_position >= start), logits, MASKED
            )
            scores[keys, :] = logits
            return jnp.maximum(peak, jnp.max(logits.reshape(-1, 8, block), axis=0))

        peak8 = lax.fori_loop(
            0, blocks_of(there), score_step, jnp.full((8, block), MASKED, F32)
        )
        peak = jnp.max(peak8, axis=0, keepdims=True)

        def weight_step(index, state):
            total, mixed = state
            keys = aligned(index, key_block)
            weight = jnp.exp2(scores[keys, :] - peak)
            weight_low = weight.astype(BF16)
            weights[there, keys, :] = weight_low
            total = total + jnp.sum(weight.reshape(-1, 8, block), axis=0)
            return total, mixed + dot(value_t[:, keys], weight_low)

        total8, mixed = lax.fori_loop(
            0,
            blocks_of(there),
            weight_step,
            (jnp.zeros((8, block), F32), jnp.zeros((HEAD, block), F32)),
        )
        inverse = 1.0 / jnp.sum(total8, axis=0, keepdims=True)
        stats[there] = jnp.broadcast_to(inverse, (8, block))
        out_all[place, :] = jnp.transpose((mixed * inverse).astype(BF16))
        for part in range(2):
            dest = 2 * there + part

            @pl.when(dest != me)
            def _():
                out_move.copy(dest, me).start()

    columns[0].every(forward_step)
    out_move.own().start()
    gradient_move.wait_recv()
    key_sum[...] = jnp.zeros_like(key_sum)
    value_sum[...] = jnp.zeros_like(value_sum)
    up_sum[...] = jnp.zeros_like(up_sum)

    key_x, value_x, grad_x, key_z, value_z, grad_z, grad_gather, grad_share = columns[8:16]

    def backward_step(step):
        there = planes - 1 - step
        place = aligned(there, block)
        slot_row, low_spread = slots_of(there, low_all)
        queries = queries_all[place, :]
        gradient_t = jnp.transpose(gradient_all[place, :]).astype(F32) * stats[there, 0:1, :]
        out_t = jnp.transpose(out_all[place, :]).astype(F32)
        delta = jnp.sum(gradient_t * out_t, axis=0, keepdims=True)
        gradient_low = jnp.transpose(gradient_t.astype(BF16))

        def back_step(index, query_sum):
            keys = aligned(index, key_block)
            weight_low = weights[there, keys, :]
            value_sum[keys, :] += dot(weight_low, gradient_low)
            dprobs = dot_nt(value_all[keys, :], gradient_low)
            dscores = (weight_low.astype(F32) * (dprobs - delta)).astype(BF16)
            key_sum[keys, :] += dot(dscores, queries)
            return query_sum + dot(key_t[:, keys], dscores)

        query_sum = lax.fori_loop(
            0, blocks_of(there), back_step, jnp.zeros((HEAD, block), F32)
        )
        query_grad = (query_sum * SCALE).astype(BF16)
        each = dot(up_picked[...], query_grad)
        low = fold_slots(slot_row, each, picks).astype(BF16)
        grad_part[there, 0] = low[:, :rows]
        grad_part[there, 1] = low[:, rows:]
        up_sum[...] += dot_nt(low_spread, query_grad)
        for part in range(2):
            half = aligned(2 * there + part, rows)
            key_out[there, part] = (key_sum[half, :] * SCALE).astype(BF16)
            value_out[there, part] = value_sum[half, :].astype(BF16)
        grad_x.to_twin(grad_part.at[there, other], grad_pair.at[there], there)
        key_x.to_twin(key_out.at[there, other], key_pair.at[there], there)
        value_x.to_twin(value_out.at[there, other], value_pair.at[there], there)

        @pl.when(step > 0)
        def _():
            pass_on(there + 1)

    def pass_on(there):
        for pair_column, column, part, pair, total, recv_ref in (
            (grad_x, grad_z, grad_part, grad_pair, grad_sum, grad_recv),
            (key_x, key_z, key_out, key_pair, key_mid, key_recv),
            (value_x, value_z, value_out, value_pair, value_mid, value_recv),
        ):
            pair_column.got(pair.at[there], there)
            total[there] = (
                part[there, side].astype(F32) + pair[there].astype(F32)
            ).astype(BF16)

            @pl.when(there != plane)
            def _():
                column.to_plane(total.at[there], recv_ref.at[plane], there)

    loop(0, planes, backward_step)
    pass_on(0)

    tenants = [adapters[own_seq, pick] for pick in range(picks)]

    def build_table(total_ref, table_ref):
        def table_step(tenant):
            total = jnp.zeros((RANK, total_ref.shape[1]), F32)
            for pick in range(picks):
                here = (tenants[pick] == tenant).astype(F32)
                total = total + total_ref[pick * RANK : (pick + 1) * RANK, :] * here
            table_ref[tenant] = total.astype(BF16)

        loop(0, seq_count, table_step)

    build_table(up_sum, up_table)
    up_back.start()
    grad_all[me] = finish_column(grad_z, grad_sum, grad_recv)
    gather_start(grad_gather, grad_share, grad_all)
    gather_finish(grad_gather, grad_share, grad_all)
    down_sum[...] = jnp.zeros_like(down_sum)

    def down_step(there):
        _, spread = slots_of(there, grad_all)
        down_sum[...] += dot(spread, tokens_all[aligned(there, block), :])

    loop(0, planes, down_step)
    build_table(down_sum, down_table)
    down_back.start()

    members = group // 2
    for column, total, recv_ref, grad in (
        (key_z, key_mid, key_recv, key_grad),
        (value_z, value_mid, value_recv, value_grad),
    ):
        recv_ref[plane] = total[plane]
        column.others(
            lambda there, column=column, recv_ref=recv_ref: column.got(recv_ref.at[there], there)
        )
        for head in range(planes // members):
            acc = recv_ref[head * members].astype(F32)
            for member in range(1, members):
                acc = acc + recv_ref[head * members + member].astype(F32)
            grad[:, head * HEAD : (head + 1) * HEAD] = acc

    def add_up(recv_ref, grad):
        grad[...] = lax.fori_loop(
            0,
            seq_count,
            lambda index, acc: acc + recv_ref[index].astype(F32),
            jnp.zeros(grad.shape, F32),
        )

    up_back.wait_recv()
    add_up(up_recv, up_grad)
    out_move.wait_recv()
    down_back.wait_recv()
    add_up(down_recv, down_grad)

    for move in (
        x_move,
        meta_move,
        base_move,
        gradient_move,
        out_move,
        down_move,
        up_move,
        up_back,
        down_back,
    ):
        move.wait_send()
    for source, target, column, share, _ in both:
        column.others(
            lambda there, source=source, column=column: column.sent(
                source.at[:, head_of(there)], there
            )
        )
        share.every(
            lambda there, target=target, share=share: share.sent(
                target.at[aligned(2 * there + side, rows), :], there
            )
        )
    for pair_column, part in (
        (low_pair_column, low_part),
        (grad_x, grad_part),
        (key_x, key_out),
        (value_x, value_out),
    ):
        pair_column.every(
            lambda there, pair_column=pair_column, part=part: pair_column.sent(
                part.at[there, other], there
            )
        )
    for column, total in (
        (low_column, low_sum),
        (grad_z, grad_sum),
        (key_z, key_mid),
        (value_z, value_mid),
    ):
        column.others(
            lambda there, column=column, total=total: column.sent(total.at[there], there)
        )
    for column, share, all_ref in (
        (low_gather, low_share, low_all),
        (grad_gather, grad_share, grad_all),
    ):
        column.others(lambda there, column=column, all_ref=all_ref: column.sent(all_ref.at[me], there))
        share.every(
            lambda there, share=share, all_ref=all_ref: share.sent(
                all_ref.at[2 * there + side], there
            )
        )


def vmem():
    return pl.BlockSpec(memory_space=pltpu.VMEM)


def hbm():
    return pl.BlockSpec(memory_space=pltpu.HBM)


def smem():
    return pl.BlockSpec(memory_space=pltpu.SMEM)


def per_device(
    normed_hidden_input,
    frozen_query_base,
    key_head_states,
    value_head_states,
    document_numbers,
    tenant_block_entry,
    sequence_adapter_list,
    adapter_down_weight,
    adapter_up_weight,
    output_gradient,
):
    ctx_count = lax.axis_size("ctx")
    seq_count = lax.axis_size("seq")
    planes = ctx_count // 2
    rows = normed_hidden_input.shape[1]
    length = rows * ctx_count
    width = adapter_down_weight.shape[2]
    picks = sequence_adapter_list.shape[1]
    key_heads = key_head_states.shape[2] // HEAD
    group = ctx_count // key_heads
    stacked = picks * RANK
    token_slots = jnp.repeat(tenant_block_entry, TB, axis=1)
    meta = jnp.pad(jnp.concatenate([document_numbers, token_slots], axis=0), ((0, 6), (0, 0)))

    def shape(dims, dtype=BF16):
        return jax.ShapeDtypeStruct(dims, dtype)

    head_rows = pltpu.VMEM((length, HEAD), BF16)
    low_plane = pltpu.VMEM((planes, RANK, rows), BF16)
    low_halves = pltpu.VMEM((planes, 2, RANK, rows), BF16)
    low_blocks = pltpu.VMEM((ctx_count, RANK, rows), BF16)
    low_buffers = [low_halves, low_plane, low_plane, low_plane, low_blocks]
    key_plane = pltpu.VMEM((planes, rows, HEAD), BF16)
    key_buffers = [pltpu.VMEM((planes, 2, rows, HEAD), BF16), key_plane, key_plane, key_plane]
    attention, key_grad, value_grad, down_grad, up_grad = pl.pallas_call(
        functools.partial(fused_kernel, ctx_count, seq_count, group),
        name="attention_layer",
        out_shape=(
            shape((rows, ctx_count * HEAD)),
            shape((rows, key_heads * HEAD), F32),
            shape((rows, key_heads * HEAD), F32),
            shape((RANK, width), F32),
            shape((RANK, HEAD), F32),
        ),
        in_specs=[hbm()] * 8 + [smem()],
        out_specs=(hbm(), vmem(), vmem(), vmem(), vmem()),
        scratch_shapes=[
            pltpu.VMEM((length, width), BF16),
            head_rows,
            head_rows,
            head_rows,
            head_rows,
            pltpu.VMEM((8, length), jnp.int32),
            pltpu.VMEM((seq_count, RANK, width), BF16),
            pltpu.VMEM((seq_count, RANK, HEAD), BF16),
            pltpu.VMEM((stacked, width), BF16),
            pltpu.VMEM((stacked, HEAD), BF16),
            pltpu.VMEM((HEAD, stacked), BF16),
            *low_buffers,
            *low_buffers,
            head_rows,
            head_rows,
            pltpu.VMEM((planes, length, 2 * rows), BF16),
            pltpu.VMEM((length, 2 * rows), F32),
            pltpu.VMEM((planes, 8, 2 * rows), F32),
            pltpu.VMEM((HEAD, length), BF16),
            pltpu.VMEM((HEAD, length), BF16),
            pltpu.VMEM((length, HEAD), F32),
            pltpu.VMEM((length, HEAD), F32),
            *key_buffers,
            *key_buffers,
            pltpu.VMEM((stacked, HEAD), F32),
            pltpu.VMEM((seq_count, RANK, HEAD), BF16),
            pltpu.VMEM((seq_count, RANK, HEAD), BF16),
            pltpu.VMEM((stacked, width), F32),
            pltpu.VMEM((seq_count, RANK, width), BF16),
            pltpu.VMEM((seq_count, RANK, width), BF16),
            pltpu.SemaphoreType.DMA((5, ctx_count)),
            pltpu.SemaphoreType.DMA((5, ctx_count)),
            pltpu.SemaphoreType.DMA((16, planes)),
            pltpu.SemaphoreType.DMA((16, planes)),
            pltpu.SemaphoreType.DMA((4, seq_count)),
            pltpu.SemaphoreType.DMA((4, seq_count)),
            pltpu.SemaphoreType.DMA((11,)),
        ],
        compiler_params=pltpu.CompilerParams(
            collective_id=0, has_side_effects=True, vmem_limit_bytes=56 << 20
        ),
    )(
        normed_hidden_input[0],
        frozen_query_base[0],
        key_head_states[0],
        value_head_states[0],
        output_gradient[0],
        meta,
        adapter_down_weight[0],
        adapter_up_weight[0],
        sequence_adapter_list,
    )
    return (
        attention[None],
        key_grad[None],
        value_grad[None],
        down_grad[None],
        up_grad[None],
    )


def solution(mesh):
    in_specs = (
        P("seq", "ctx", None),
        P("seq", "ctx", None),
        P("seq", "ctx", None),
        P("seq", "ctx", None),
        P("seq", "ctx"),
        P("seq", "ctx"),
        P(),
        P("seq", None, "ctx"),
        P("seq", None, "ctx"),
        P("seq", "ctx", None),
    )
    out_specs = (
        P("seq", "ctx", None),
        P("seq", "ctx", None),
        P("seq", "ctx", None),
        P("seq", None, "ctx"),
        P("seq", None, "ctx"),
    )
    return jax.shard_map(
        per_device, mesh=mesh, in_specs=in_specs, out_specs=out_specs, check_vma=False
    )
```

```python
import functools
import math

import jax
import jax.numpy as jnp
from jax import lax
from jax.experimental import pallas as pl
from jax.experimental.pallas import tpu as pltpu
from jax.sharding import PartitionSpec as P

MESH = pl.DeviceIdType.MESH
BF16 = jnp.bfloat16
F32 = jnp.float32
HEAD = 128
RANK = 64
TB = 32
KEY_BLOCK = 512
MASKED = -1e30
SCALE = 1.0 / math.sqrt(HEAD)
LOG2E = math.log2(math.e)


def dot(a, b):
    return lax.dot_general(a, b, (((1,), (0,)), ((), ())), preferred_element_type=F32)


def dot_nt(a, b):
    return lax.dot_general(a, b, (((1,), (1,)), ((), ())), preferred_element_type=F32)


def aligned(index, size):
    return pl.ds(pl.multiple_of(index * size, size), size)


def push(source, target, send, recv, dest):
    return pltpu.make_async_remote_copy(
        src_ref=source,
        dst_ref=target,
        send_sem=send,
        recv_sem=recv,
        device_id=dest,
        device_id_type=MESH,
    )


def loop(low, high, body):
    def step(index, carry):
        body(index)
        return carry

    lax.fori_loop(low, high, step, 0)


class Exchange:
    def __init__(self, axis, count, me, source, target, send, recv, local):
        self.axis, self.count, self.me = axis, count, me
        self.source, self.target = source, target
        self.send, self.recv, self.local = send, recv, local

    def copy(self, peer, place):
        return push(
            self.source(peer),
            self.target(place),
            self.send.at[peer],
            self.recv.at[place],
            {self.axis: peer},
        )

    def own(self):
        return pltpu.make_async_copy(self.source(self.me), self.target(self.me), self.local)

    def each(self, body):
        loop(1, self.count, lambda shift: body(lax.rem(self.me + shift, self.count)))

    def start(self):
        self.each(lambda peer: self.copy(peer, self.me).start())
        if self.local is not None:
            self.own().start()

    def wait_from(self, place):
        self.copy(place, place).wait_recv()

    def wait_recv(self):
        loop(
            1,
            self.count,
            lambda shift: self.wait_from(lax.rem(self.me + self.count - shift, self.count)),
        )
        if self.local is not None:
            self.own().wait()

    def wait_send(self):
        self.each(lambda peer: self.copy(peer, self.me).wait_send())


class Column:
    def __init__(self, planes, plane, side, send, recv):
        self.planes, self.plane, self.side = planes, plane, side
        self.send, self.recv = send, recv

    def to_plane(self, source, target, there):
        dest = {"ctx": there * 2 + self.side}
        push(source, target, self.send.at[there], self.recv.at[self.plane], dest).start()

    def to_twin(self, source, target, index):
        dest = {"ctx": self.plane * 2 + 1 - self.side}
        push(source, target, self.send.at[index], self.recv.at[index], dest).start()

    def got(self, target, index):
        dest = {"ctx": self.plane * 2 + 1 - self.side}
        push(target, target, self.send.at[index], self.recv.at[index], dest).wait_recv()

    def sent(self, source, index):
        dest = {"ctx": self.plane * 2 + 1 - self.side}
        push(source, source, self.send.at[index], self.recv.at[index], dest).wait_send()

    def others(self, body):
        loop(1, self.planes, lambda shift: body(lax.rem(self.plane + shift, self.planes)))

    def every(self, body):
        loop(0, self.planes, lambda shift: body(lax.rem(self.plane + shift, self.planes)))

    def away(self, step):
        left = self.planes - step
        shift = jnp.where(lax.rem(left, 2) == 0, left // 2, -(left // 2))
        return lax.rem(self.plane + self.planes + shift, self.planes)

    def arrivals(self, body, first=0):
        loop(
            first,
            self.planes,
            lambda shift: body(lax.rem(self.plane + self.planes - shift, self.planes)),
        )


def meet(me_ctx, ctx_count, me_seq, seq_count):
    barrier = pltpu.get_barrier_semaphore()

    def greet(axis, me, count):
        def step(shift):
            pl.semaphore_signal(
                barrier,
                inc=1,
                device_id={axis: lax.rem(me + shift, count)},
                device_id_type=MESH,
            )

        loop(1, count, step)

    greet("ctx", me_ctx, ctx_count)
    greet("seq", me_seq, seq_count)
    pl.semaphore_wait(barrier, ctx_count + seq_count - 2)


def spread_slots(slot_row, low, picks):
    zero = jnp.zeros_like(low)
    return jnp.concatenate(
        [jnp.where(slot_row == pick, low, zero) for pick in range(picks)], axis=0
    )


def fold_slots(slot_row, each, picks):
    total = jnp.zeros((RANK, each.shape[1]), F32)
    for pick in range(picks):
        part = each[pick * RANK : (pick + 1) * RANK]
        total = total + jnp.where(slot_row == pick, part, 0.0)
    return total


def fused_kernel(
    ctx_count,
    seq_count,
    group,
    tokens,
    base,
    key,
    value,
    gradient,
    meta,
    down,
    up,
    adapters,
    attention,
    key_grad,
    value_grad,
    down_grad,
    up_grad,
    tokens_all,
    base_all,
    key_all,
    value_all,
    gradient_all,
    meta_all,
    down_tenants,
    up_tenants,
    down_picked,
    up_picked,
    up_t,
    low_part,
    low_recv,
    low_all,
    grad_part,
    grad_recv,
    grad_all,
    queries_all,
    out_all,
    weights,
    dscores_all,
    scores,
    stats,
    key_t,
    value_t,
    key_out,
    key_pair,
    key_mid,
    key_recv,
    value_out,
    value_pair,
    value_mid,
    value_recv,
    up_sum,
    up_table,
    up_recv,
    down_sum,
    down_table,
    down_recv,
    send,
    recv,
    send_z,
    recv_z,
    send_seq,
    recv_seq,
    local,
):
    me = lax.axis_index("ctx")
    own_seq = lax.axis_index("seq")
    planes = ctx_count // 2
    plane, side = me // 2, lax.rem(me, 2)
    other = 1 - side
    rows = tokens.shape[0]
    block = 2 * rows
    length = tokens_all.shape[0]
    width = tokens_all.shape[1]
    picks = adapters.shape[1]
    key_block = min(KEY_BLOCK, length)

    def over_ctx(slot, source, target, has_own=True):
        return Exchange(
            "ctx",
            ctx_count,
            me,
            source,
            target,
            send.at[slot],
            recv.at[slot],
            local.at[slot] if has_own else None,
        )

    def over_seq(slot, source, target):
        return Exchange(
            "seq",
            seq_count,
            own_seq,
            source,
            target,
            send_seq.at[slot],
            recv_seq.at[slot],
            local.at[5 + slot],
        )

    columns = [
        Column(planes, plane, side, send_z.at[slot], recv_z.at[slot])
        for slot in range(send_z.shape[0])
    ]
    x_move = over_ctx(
        0,
        lambda peer: tokens.at[:, aligned(peer, width)],
        lambda place: tokens_all.at[aligned(place, rows), :],
    )
    meta_move = over_ctx(
        1, lambda peer: meta, lambda place: meta_all.at[:, aligned(place, rows)]
    )
    base_move = over_ctx(
        2,
        lambda peer: base.at[:, aligned(peer, HEAD)],
        lambda place: base_all.at[aligned(place, rows), :],
    )
    gradient_move = over_ctx(
        3,
        lambda peer: gradient.at[:, aligned(peer, HEAD)],
        lambda place: gradient_all.at[aligned(place, rows), :],
    )
    out_move = over_ctx(
        4,
        lambda peer: out_all.at[aligned(peer, rows), :],
        lambda place: attention.at[:, aligned(place, HEAD)],
    )
    grad_move = over_ctx(
        5, lambda peer: grad_part.at[peer], lambda place: grad_recv.at[place], has_own=False
    )
    grad_gather = over_ctx(
        6, lambda peer: grad_all.at[me], lambda place: grad_all.at[place], has_own=False
    )
    low_move = over_ctx(
        7, lambda peer: low_part.at[peer], lambda place: low_recv.at[place], has_own=False
    )
    low_gather = over_ctx(
        8, lambda peer: low_all.at[me], lambda place: low_all.at[place], has_own=False
    )
    down_move = over_seq(0, lambda peer: down, lambda place: down_tenants.at[place])
    up_move = over_seq(1, lambda peer: up, lambda place: up_tenants.at[place])
    up_back = over_seq(2, lambda peer: up_table.at[peer], lambda place: up_recv.at[place])
    down_back = over_seq(3, lambda peer: down_table.at[peer], lambda place: down_recv.at[place])
    both = (
        (key, key_all, columns[0], columns[1], local.at[9]),
        (value, value_all, columns[2], columns[3], local.at[10]),
    )

    meet(me, ctx_count, own_seq, seq_count)

    def head_of(there):
        return aligned((2 * there) // group, HEAD)

    def own_rows():
        return aligned(me, rows)

    def key_send():
        for source, target, column, _, own_sem in both:
            column.others(
                lambda there, source=source, target=target, column=column: column.to_plane(
                    source.at[:, head_of(there)], target.at[own_rows(), :], there
                )
            )
            pltpu.make_async_copy(
                source.at[:, head_of(plane)], target.at[own_rows(), :], own_sem
            ).start()

    def key_forward():
        for source, target, column, share, own_sem in both:
            pltpu.make_async_copy(
                source.at[:, head_of(plane)], target.at[own_rows(), :], own_sem
            ).wait()

            def forward(there, target=target, column=column, share=share):
                place = target.at[aligned(2 * there + side, rows), :]

                @pl.when(there != plane)
                def _():
                    column.got(place, there)

                share.to_twin(place, place, there)

            column.arrivals(forward)

    down_move.start()
    meta_move.start()
    x_move.start()
    up_move.start()
    base_move.start()

    meta_move.wait_recv()
    down_move.wait_recv()
    for pick in range(picks):
        down_picked[pick * RANK : (pick + 1) * RANK, :] = down_tenants[adapters[own_seq, pick]]

    x_move.own().wait()

    def deal(low, there, part_ref, move):
        for part in range(2):
            dest = 2 * there + part
            part_ref[dest] = low[:, part * rows : (part + 1) * rows]

            @pl.when(dest != me)
            def _():
                move.copy(dest, me).start()

    def collect(part_ref, recv_ref, all_ref, move, gather):
        recv_ref[me] = part_ref[me]
        move.wait_recv()
        all_ref[me] = lax.fori_loop(
            0,
            ctx_count,
            lambda place, acc: acc + recv_ref[place].astype(F32),
            jnp.zeros((RANK, rows), F32),
        ).astype(BF16)
        gather.start()

    def low_step(there):
        for part in range(2):
            place = 2 * there + part

            @pl.when(place != me)
            def _():
                x_move.wait_from(place)

        cols = aligned(there, block)
        each = dot_nt(down_picked[...], tokens_all[cols, :])
        low = fold_slots(meta_all[1:2, cols], each, picks).astype(BF16)
        deal(low, there, low_part, low_move)

    columns[0].arrivals(low_step)
    key_send()

    collect(low_part, low_recv, low_all, low_move, low_gather)
    key_forward()
    low_gather.wait_recv()
    up_move.wait_recv()
    for pick in range(picks):
        up_picked[pick * RANK : (pick + 1) * RANK, :] = up_tenants[adapters[own_seq, pick]]
    up_t[...] = jnp.transpose(up_picked[...])
    for source, target, column, share, own_sem in both:
        share.every(
            lambda there, target=target, share=share: share.got(
                target.at[aligned(2 * there + other, rows), :], there
            )
        )
    key_t[...] = jnp.transpose(key_all[...])
    value_t[...] = jnp.transpose(value_all[...])
    base_move.wait_recv()

    documents = meta_all[0:1, :]
    cuts = [
        jnp.sum(jnp.where(documents < number, 1, 0), axis=1, keepdims=True) for number in (1, 2, 3)
    ]

    def slots_of(there, all_ref):
        slot_row = meta_all[1:2, aligned(there, block)]
        low = jnp.concatenate([all_ref[2 * there], all_ref[2 * there + 1]], axis=1)
        return slot_row, spread_slots(slot_row, low, picks)

    def blocks_of(there):
        return (there * block + block - 1) // key_block + 1

    def forward_step(there):
        place = aligned(there, block)
        _, low_spread = slots_of(there, low_all)
        lifted = dot(up_t[...], low_spread)
        queries = (base_all[place, :].astype(F32) + jnp.transpose(lifted)).astype(BF16)
        queries_all[place, :] = queries
        position = there * block + lax.broadcasted_iota(jnp.int32, (1, block), 1)
        start = jnp.zeros((1, block), jnp.int32)
        for cut in cuts:
            start = jnp.where(position >= cut, cut, start)

        def score_step(index, peak):
            keys = aligned(index, key_block)
            logits = dot_nt(key_all[keys, :], queries) * (SCALE * LOG2E)
            key_position = index * key_block + lax.broadcasted_iota(
                jnp.int32, (key_block, block), 0
            )
            logits = jnp.where(
                (key_position <= position) & (key_position >= start), logits, MASKED
            )
            scores[keys, :] = logits
            return jnp.maximum(peak, jnp.max(logits.reshape(-1, 8, block), axis=0))

        peak8 = lax.fori_loop(
            0, blocks_of(there), score_step, jnp.full((8, block), MASKED, F32)
        )
        peak = jnp.max(peak8, axis=0, keepdims=True)

        def weight_step(index, state):
            total, mixed = state
            keys = aligned(index, key_block)
            weight = jnp.exp2(scores[keys, :] - peak)
            weight_low = weight.astype(BF16)
            weights[there, keys, :] = weight_low
            total = total + jnp.sum(weight.reshape(-1, 8, block), axis=0)
            return total, mixed + dot(value_t[:, keys], weight_low)

        total8, mixed = lax.fori_loop(
            0,
            blocks_of(there),
            weight_step,
            (jnp.zeros((8, block), F32), jnp.zeros((HEAD, block), F32)),
        )
        inverse = 1.0 / jnp.sum(total8, axis=0, keepdims=True)
        stats[there] = jnp.broadcast_to(inverse, (8, block))
        out_all[place, :] = jnp.transpose((mixed * inverse).astype(BF16))
        for part in range(2):
            dest = 2 * there + part

            @pl.when(dest != me)
            def _():
                out_move.copy(dest, me).start()

    gradient_move.start()
    loop(0, planes, lambda step: forward_step(columns[0].away(step)))
    out_move.own().start()
    gradient_move.wait_recv()
    up_sum[...] = jnp.zeros_like(up_sum)

    def backward_step(there):
        place = aligned(there, block)
        slot_row, low_spread = slots_of(there, low_all)
        gradient_t = jnp.transpose(gradient_all[place, :]).astype(F32) * stats[there, 0:1, :]
        out_t = jnp.transpose(out_all[place, :]).astype(F32)
        delta = jnp.sum(gradient_t * out_t, axis=0, keepdims=True)
        gradient_low = jnp.transpose(gradient_t.astype(BF16))
        gradient_all[place, :] = gradient_low

        def back_step(index, query_sum):
            keys = aligned(index, key_block)
            dprobs = dot_nt(value_all[keys, :], gradient_low)
            dscores = (weights[there, keys, :].astype(F32) * (dprobs - delta)).astype(BF16)
            dscores_all[there, keys, :] = dscores
            return query_sum + dot(key_t[:, keys], dscores)

        query_sum = lax.fori_loop(
            0, blocks_of(there), back_step, jnp.zeros((HEAD, block), F32)
        )
        query_grad = (query_sum * SCALE).astype(BF16)
        each = dot(up_picked[...], query_grad)
        low = fold_slots(slot_row, each, picks).astype(BF16)
        deal(low, there, grad_part, grad_move)
        up_sum[...] += dot_nt(low_spread, query_grad)

    loop(0, planes, lambda step: backward_step(columns[0].away(step)))

    tenants = [adapters[own_seq, pick] for pick in range(picks)]

    def build_table(total_ref, table_ref):
        def table_step(tenant):
            total = jnp.zeros((RANK, total_ref.shape[1]), F32)
            for pick in range(picks):
                here = (tenants[pick] == tenant).astype(F32)
                total = total + total_ref[pick * RANK : (pick + 1) * RANK, :] * here
            table_ref[tenant] = total.astype(BF16)

        loop(0, seq_count, table_step)

    build_table(up_sum, up_table)
    up_back.start()

    key_x, value_x, key_z, value_z = columns[4:8]

    def key_step(shift):
        there = key_x.away(shift)
        place = aligned(there, block)

        def query_step(index, state):
            keys_acc, values_acc = state
            from_rows = aligned(index, block)
            values_acc = values_acc + dot(weights[index, place, :], gradient_all[from_rows, :])
            keys_acc = keys_acc + dot(dscores_all[index, place, :], queries_all[from_rows, :])
            return keys_acc, values_acc

        zero = jnp.zeros((block, HEAD), F32)
        keys_acc, values_acc = lax.fori_loop(there, planes, query_step, (zero, zero))
        keys_low = (keys_acc * SCALE).astype(BF16)
        values_low = values_acc.astype(BF16)
        for part in range(2):
            key_out[there, part] = keys_low[part * rows : (part + 1) * rows]
            value_out[there, part] = values_low[part * rows : (part + 1) * rows]
        key_x.to_twin(key_out.at[there, other], key_pair.at[there], there)
        value_x.to_twin(value_out.at[there, other], value_pair.at[there], there)

        @pl.when(shift > 0)
        def _():
            pass_on(key_x.away(shift - 1))

    def pass_on(there):
        for pair_column, column, part, pair, total, recv_ref in (
            (key_x, key_z, key_out, key_pair, key_mid, key_recv),
            (value_x, value_z, value_out, value_pair, value_mid, value_recv),
        ):
            pair_column.got(pair.at[there], there)
            total[there] = (
                part[there, side].astype(F32) + pair[there].astype(F32)
            ).astype(BF16)

            @pl.when(there != plane)
            def _():
                column.to_plane(total.at[there], recv_ref.at[plane], there)

    first_cut, second_cut = planes // 4, 3 * planes // 4
    loop(0, first_cut, key_step)
    collect(grad_part, grad_recv, grad_all, grad_move, grad_gather)
    loop(first_cut, second_cut, key_step)
    grad_gather.wait_recv()
    down_sum[...] = jnp.zeros_like(down_sum)

    def down_step(there):
        _, spread = slots_of(there, grad_all)
        down_sum[...] += dot(spread, tokens_all[aligned(there, block), :])

    loop(0, planes, down_step)
    build_table(down_sum, down_table)
    down_back.start()
    loop(second_cut, planes, key_step)
    pass_on(plane)

    members = group // 2
    for column, total, recv_ref, grad in (
        (key_z, key_mid, key_recv, key_grad),
        (value_z, value_mid, value_recv, value_grad),
    ):
        recv_ref[plane] = total[plane]
        column.others(
            lambda there, column=column, recv_ref=recv_ref: column.got(recv_ref.at[there], there)
        )
        for head in range(planes // members):
            acc = recv_ref[head * members].astype(F32)
            for member in range(1, members):
                acc = acc + recv_ref[head * members + member].astype(F32)
            grad[:, head * HEAD : (head + 1) * HEAD] = acc

    def add_up(recv_ref, grad):
        grad[...] = lax.fori_loop(
            0,
            seq_count,
            lambda index, acc: acc + recv_ref[index].astype(F32),
            jnp.zeros(grad.shape, F32),
        )

    up_back.wait_recv()
    add_up(up_recv, up_grad)
    out_move.wait_recv()
    down_back.wait_recv()
    add_up(down_recv, down_grad)

    for move in (
        x_move,
        meta_move,
        base_move,
        gradient_move,
        out_move,
        down_move,
        up_move,
        up_back,
        down_back,
        low_move,
        low_gather,
        grad_move,
        grad_gather,
    ):
        move.wait_send()
    for source, target, column, share, _ in both:
        column.others(
            lambda there, source=source, column=column: column.sent(
                source.at[:, head_of(there)], there
            )
        )
        share.every(
            lambda there, target=target, share=share: share.sent(
                target.at[aligned(2 * there + side, rows), :], there
            )
        )
    for pair_column, part in (
        (key_x, key_out),
        (value_x, value_out),
    ):
        pair_column.every(
            lambda there, pair_column=pair_column, part=part: pair_column.sent(
                part.at[there, other], there
            )
        )
    for column, total in (
        (key_z, key_mid),
        (value_z, value_mid),
    ):
        column.others(
            lambda there, column=column, total=total: column.sent(total.at[there], there)
        )


def hand_over_kernel(*refs):
    for source, target in zip(refs[:5], refs[5:]):
        target[...] = source[...]


def vmem():
    return pl.BlockSpec(memory_space=pltpu.VMEM)


def hbm():
    return pl.BlockSpec(memory_space=pltpu.HBM)


def smem():
    return pl.BlockSpec(memory_space=pltpu.SMEM)


def per_device(
    normed_hidden_input,
    frozen_query_base,
    key_head_states,
    value_head_states,
    document_numbers,
    tenant_block_entry,
    sequence_adapter_list,
    adapter_down_weight,
    adapter_up_weight,
    output_gradient,
):
    ctx_count = lax.axis_size("ctx")
    seq_count = lax.axis_size("seq")
    planes = ctx_count // 2
    rows = normed_hidden_input.shape[1]
    length = rows * ctx_count
    width = adapter_down_weight.shape[2]
    picks = sequence_adapter_list.shape[1]
    key_heads = key_head_states.shape[2] // HEAD
    group = ctx_count // key_heads
    stacked = picks * RANK
    token_slots = jnp.repeat(tenant_block_entry, TB, axis=1)
    meta = jnp.pad(jnp.concatenate([document_numbers, token_slots], axis=0), ((0, 6), (0, 0)))

    def shape(dims, dtype=BF16):
        return jax.ShapeDtypeStruct(dims, dtype)

    head_rows = pltpu.VMEM((length, HEAD), BF16)
    low_blocks = pltpu.VMEM((ctx_count, RANK, rows), BF16)
    key_plane = pltpu.VMEM((planes, rows, HEAD), BF16)
    key_buffers = [pltpu.VMEM((planes, 2, rows, HEAD), BF16), key_plane, key_plane, key_plane]
    attention, key_grad, value_grad, down_grad, up_grad = pl.pallas_call(
        functools.partial(fused_kernel, ctx_count, seq_count, group),
        name="attention_layer",
        out_shape=(
            shape((rows, ctx_count * HEAD)),
            shape((rows, key_heads * HEAD), F32),
            shape((rows, key_heads * HEAD), F32),
            shape((RANK, width), F32),
            shape((RANK, HEAD), F32),
        ),
        in_specs=[hbm()] * 8 + [smem()],
        out_specs=(hbm(), vmem(), vmem(), vmem(), vmem()),
        scratch_shapes=[
            pltpu.VMEM((length, width), BF16),
            head_rows,
            head_rows,
            head_rows,
            head_rows,
            pltpu.VMEM((8, length), jnp.int32),
            pltpu.VMEM((seq_count, RANK, width), BF16),
            pltpu.VMEM((seq_count, RANK, HEAD), BF16),
            pltpu.VMEM((stacked, width), BF16),
            pltpu.VMEM((stacked, HEAD), BF16),
            pltpu.VMEM((HEAD, stacked), BF16),
            *[low_blocks] * 6,
            head_rows,
            head_rows,
            pltpu.VMEM((planes, length, 2 * rows), BF16),
            pltpu.VMEM((planes, length, 2 * rows), BF16),
            pltpu.VMEM((length, 2 * rows), F32),
            pltpu.VMEM((planes, 8, 2 * rows), F32),
            pltpu.VMEM((HEAD, length), BF16),
            pltpu.VMEM((HEAD, length), BF16),
            *key_buffers,
            *key_buffers,
            pltpu.VMEM((stacked, HEAD), F32),
            pltpu.VMEM((seq_count, RANK, HEAD), BF16),
            pltpu.VMEM((seq_count, RANK, HEAD), BF16),
            pltpu.VMEM((stacked, width), F32),
            pltpu.VMEM((seq_count, RANK, width), BF16),
            pltpu.VMEM((seq_count, RANK, width), BF16),
            pltpu.SemaphoreType.DMA((9, ctx_count)),
            pltpu.SemaphoreType.DMA((9, ctx_count)),
            pltpu.SemaphoreType.DMA((8, planes)),
            pltpu.SemaphoreType.DMA((8, planes)),
            pltpu.SemaphoreType.DMA((4, seq_count)),
            pltpu.SemaphoreType.DMA((4, seq_count)),
            pltpu.SemaphoreType.DMA((11,)),
        ],
        compiler_params=pltpu.CompilerParams(
            collective_id=0, has_side_effects=True, vmem_limit_bytes=56 << 20
        ),
    )(
        normed_hidden_input[0],
        frozen_query_base[0],
        key_head_states[0],
        value_head_states[0],
        output_gradient[0],
        meta,
        adapter_down_weight[0],
        adapter_up_weight[0],
        sequence_adapter_list,
    )
    attention, key_grad, value_grad, down_grad, up_grad = pl.pallas_call(
        hand_over_kernel,
        name="hand_over",
        out_shape=tuple(
            shape(array.shape, array.dtype)
            for array in (attention, key_grad, value_grad, down_grad, up_grad)
        ),
        in_specs=[vmem()] * 5,
        out_specs=(vmem(),) * 5,
    )(attention, key_grad, value_grad, down_grad, up_grad)
    return (
        attention[None],
        key_grad[None],
        value_grad[None],
        down_grad[None],
        up_grad[None],
    )


def solution(mesh):
    in_specs = (
        P("seq", "ctx", None),
        P("seq", "ctx", None),
        P("seq", "ctx", None),
        P("seq", "ctx", None),
        P("seq", "ctx"),
        P("seq", "ctx"),
        P(),
        P("seq", None, "ctx"),
        P("seq", None, "ctx"),
        P("seq", "ctx", None),
    )
    out_specs = (
        P("seq", "ctx", None),
        P("seq", "ctx", None),
        P("seq", "ctx", None),
        P("seq", None, "ctx"),
        P("seq", None, "ctx"),
    )
    return jax.shard_map(
        per_device, mesh=mesh, in_specs=in_specs, out_specs=out_specs, check_vma=False
    )
```

```python
import functools
import math

import jax
import jax.numpy as jnp
from jax import lax
from jax.experimental import pallas as pl
from jax.experimental.pallas import tpu as pltpu
from jax.sharding import PartitionSpec as P

MESH = pl.DeviceIdType.MESH
BF16 = jnp.bfloat16
F32 = jnp.float32
HEAD = 128
RANK = 64
TB = 32
KEY_BLOCK = 512
MASKED = -1e30
SCALE = 1.0 / math.sqrt(HEAD)
LOG2E = math.log2(math.e)


def dot(a, b):
    return lax.dot_general(a, b, (((1,), (0,)), ((), ())), preferred_element_type=F32)


def dot_nt(a, b):
    return lax.dot_general(a, b, (((1,), (1,)), ((), ())), preferred_element_type=F32)


def aligned(index, size):
    return pl.ds(pl.multiple_of(index * size, size), size)


def push(source, target, send, recv, dest):
    return pltpu.make_async_remote_copy(
        src_ref=source,
        dst_ref=target,
        send_sem=send,
        recv_sem=recv,
        device_id=dest,
        device_id_type=MESH,
    )


def loop(low, high, body):
    def step(index, carry):
        body(index)
        return carry

    lax.fori_loop(low, high, step, 0)


class Exchange:
    def __init__(self, axis, count, me, source, target, send, recv, local):
        self.axis, self.count, self.me = axis, count, me
        self.source, self.target = source, target
        self.send, self.recv, self.local = send, recv, local

    def copy(self, peer, place):
        return push(
            self.source(peer),
            self.target(place),
            self.send.at[peer],
            self.recv.at[place],
            {self.axis: peer},
        )

    def own(self):
        return pltpu.make_async_copy(self.source(self.me), self.target(self.me), self.local)

    def each(self, body):
        loop(1, self.count, lambda shift: body(lax.rem(self.me + shift, self.count)))

    def start(self):
        self.each(lambda peer: self.copy(peer, self.me).start())
        if self.local is not None:
            self.own().start()

    def wait_from(self, place):
        self.copy(place, place).wait_recv()

    def wait_recv(self):
        loop(
            1,
            self.count,
            lambda shift: self.wait_from(lax.rem(self.me + self.count - shift, self.count)),
        )
        if self.local is not None:
            self.own().wait()

    def wait_send(self):
        self.each(lambda peer: self.copy(peer, self.me).wait_send())


class Column:
    def __init__(self, planes, plane, side, send, recv):
        self.planes, self.plane, self.side = planes, plane, side
        self.send, self.recv = send, recv

    def to_plane(self, source, target, there):
        dest = {"ctx": there * 2 + self.side}
        push(source, target, self.send.at[there], self.recv.at[self.plane], dest).start()

    def to_twin(self, source, target, index):
        dest = {"ctx": self.plane * 2 + 1 - self.side}
        push(source, target, self.send.at[index], self.recv.at[index], dest).start()

    def got(self, target, index):
        dest = {"ctx": self.plane * 2 + 1 - self.side}
        push(target, target, self.send.at[index], self.recv.at[index], dest).wait_recv()

    def sent(self, source, index):
        dest = {"ctx": self.plane * 2 + 1 - self.side}
        push(source, source, self.send.at[index], self.recv.at[index], dest).wait_send()

    def others(self, body):
        loop(1, self.planes, lambda shift: body(lax.rem(self.plane + shift, self.planes)))

    def every(self, body):
        loop(0, self.planes, lambda shift: body(lax.rem(self.plane + shift, self.planes)))

    def away(self, step):
        left = self.planes - step
        shift = jnp.where(lax.rem(left, 2) == 0, left // 2, -(left // 2))
        return lax.rem(self.plane + self.planes + shift, self.planes)

    def arrivals(self, body, first=0):
        loop(
            first,
            self.planes,
            lambda shift: body(lax.rem(self.plane + self.planes - shift, self.planes)),
        )


def meet(me_ctx, ctx_count, me_seq, seq_count):
    barrier = pltpu.get_barrier_semaphore()

    def greet(axis, me, count):
        def step(shift):
            pl.semaphore_signal(
                barrier,
                inc=1,
                device_id={axis: lax.rem(me + shift, count)},
                device_id_type=MESH,
            )

        loop(1, count, step)

    greet("ctx", me_ctx, ctx_count)
    greet("seq", me_seq, seq_count)
    pl.semaphore_wait(barrier, ctx_count + seq_count - 2)


def spread_slots(slot_row, low, picks):
    zero = jnp.zeros_like(low)
    return jnp.concatenate(
        [jnp.where(slot_row == pick, low, zero) for pick in range(picks)], axis=0
    )


def fold_slots(slot_row, each, picks):
    total = jnp.zeros((RANK, each.shape[1]), F32)
    for pick in range(picks):
        part = each[pick * RANK : (pick + 1) * RANK]
        total = total + jnp.where(slot_row == pick, part, 0.0)
    return total


def fused_kernel(
    ctx_count,
    seq_count,
    group,
    tokens,
    base,
    key,
    value,
    gradient,
    meta,
    down,
    up,
    adapters,
    attention,
    key_grad,
    value_grad,
    down_grad,
    up_grad,
    tokens_all,
    base_all,
    key_all,
    value_all,
    gradient_all,
    meta_all,
    down_tenants,
    up_tenants,
    down_picked,
    up_picked,
    up_t,
    low_part,
    low_recv,
    low_all,
    grad_part,
    grad_recv,
    grad_all,
    queries_all,
    out_all,
    weights,
    dscores_all,
    scores,
    stats,
    key_t,
    value_t,
    key_out,
    key_pair,
    key_mid,
    key_recv,
    value_out,
    value_pair,
    value_mid,
    value_recv,
    up_sum,
    up_table,
    up_recv,
    down_sum,
    down_table,
    down_recv,
    send,
    recv,
    send_z,
    recv_z,
    send_seq,
    recv_seq,
    local,
):
    me = lax.axis_index("ctx")
    own_seq = lax.axis_index("seq")
    planes = ctx_count // 2
    plane, side = me // 2, lax.rem(me, 2)
    other = 1 - side
    rows = tokens.shape[0]
    block = 2 * rows
    length = tokens_all.shape[0]
    width = tokens_all.shape[1]
    picks = adapters.shape[1]
    key_block = min(KEY_BLOCK, length)

    def over_ctx(slot, source, target, has_own=True):
        return Exchange(
            "ctx",
            ctx_count,
            me,
            source,
            target,
            send.at[slot],
            recv.at[slot],
            local.at[slot] if has_own else None,
        )

    def over_seq(slot, source, target):
        return Exchange(
            "seq",
            seq_count,
            own_seq,
            source,
            target,
            send_seq.at[slot],
            recv_seq.at[slot],
            local.at[5 + slot],
        )

    columns = [
        Column(planes, plane, side, send_z.at[slot], recv_z.at[slot])
        for slot in range(send_z.shape[0])
    ]
    x_move = over_ctx(
        0,
        lambda peer: tokens.at[:, aligned(peer, width)],
        lambda place: tokens_all.at[aligned(place, rows), :],
    )
    meta_move = over_ctx(
        1, lambda peer: meta, lambda place: meta_all.at[:, aligned(place, rows)]
    )
    base_move = over_ctx(
        2,
        lambda peer: base.at[:, aligned(peer, HEAD)],
        lambda place: base_all.at[aligned(place, rows), :],
    )
    gradient_move = over_ctx(
        3,
        lambda peer: gradient.at[:, aligned(peer, HEAD)],
        lambda place: gradient_all.at[aligned(place, rows), :],
    )
    out_move = over_ctx(
        4,
        lambda peer: out_all.at[aligned(peer, rows), :],
        lambda place: attention.at[:, aligned(place, HEAD)],
    )
    grad_move = over_ctx(
        5, lambda peer: grad_part.at[peer], lambda place: grad_recv.at[place], has_own=False
    )
    grad_gather = over_ctx(
        6, lambda peer: grad_all.at[me], lambda place: grad_all.at[place], has_own=False
    )
    low_move = over_ctx(
        7, lambda peer: low_part.at[peer], lambda place: low_recv.at[place], has_own=False
    )
    low_gather = over_ctx(
        8, lambda peer: low_all.at[me], lambda place: low_all.at[place], has_own=False
    )
    down_move = over_seq(0, lambda peer: down, lambda place: down_tenants.at[place])
    up_move = over_seq(1, lambda peer: up, lambda place: up_tenants.at[place])
    up_back = over_seq(2, lambda peer: up_table.at[peer], lambda place: up_recv.at[place])
    down_back = over_seq(3, lambda peer: down_table.at[peer], lambda place: down_recv.at[place])
    both = (
        (key, key_all, columns[0], columns[1], local.at[9]),
        (value, value_all, columns[2], columns[3], local.at[10]),
    )

    meet(me, ctx_count, own_seq, seq_count)

    def head_of(there):
        return aligned((2 * there) // group, HEAD)

    def own_rows():
        return aligned(me, rows)

    def key_send():
        for source, target, column, _, own_sem in both:
            column.others(
                lambda there, source=source, target=target, column=column: column.to_plane(
                    source.at[:, head_of(there)], target.at[own_rows(), :], there
                )
            )
            pltpu.make_async_copy(
                source.at[:, head_of(plane)], target.at[own_rows(), :], own_sem
            ).start()

    def key_forward():
        for source, target, column, share, own_sem in both:
            pltpu.make_async_copy(
                source.at[:, head_of(plane)], target.at[own_rows(), :], own_sem
            ).wait()

            def forward(there, target=target, column=column, share=share):
                place = target.at[aligned(2 * there + side, rows), :]

                @pl.when(there != plane)
                def _():
                    column.got(place, there)

                share.to_twin(place, place, there)

            column.arrivals(forward)

    down_move.start()
    meta_move.start()
    x_move.start()
    up_move.start()
    base_move.start()

    meta_move.wait_recv()
    down_move.wait_recv()
    for pick in range(picks):
        down_picked[pick * RANK : (pick + 1) * RANK, :] = down_tenants[adapters[own_seq, pick]]

    x_move.own().wait()

    def deal(low, there, part_ref, move):
        for part in range(2):
            dest = 2 * there + part
            part_ref[dest] = low[:, part * rows : (part + 1) * rows]

            @pl.when(dest != me)
            def _():
                move.copy(dest, me).start()

    def collect(part_ref, recv_ref, all_ref, move, gather):
        recv_ref[me] = part_ref[me]
        move.wait_recv()
        all_ref[me] = lax.fori_loop(
            0,
            ctx_count,
            lambda place, acc: acc + recv_ref[place].astype(F32),
            jnp.zeros((RANK, rows), F32),
        ).astype(BF16)
        gather.start()

    def low_step(there):
        for part in range(2):
            place = 2 * there + part

            @pl.when(place != me)
            def _():
                x_move.wait_from(place)

        cols = aligned(there, block)
        each = dot_nt(down_picked[...], tokens_all[cols, :])
        low = fold_slots(meta_all[1:2, cols], each, picks).astype(BF16)
        deal(low, there, low_part, low_move)

    columns[0].arrivals(low_step)
    key_send()

    collect(low_part, low_recv, low_all, low_move, low_gather)
    key_forward()
    low_gather.wait_recv()
    up_move.wait_recv()
    for pick in range(picks):
        up_picked[pick * RANK : (pick + 1) * RANK, :] = up_tenants[adapters[own_seq, pick]]
    up_t[...] = jnp.transpose(up_picked[...])
    for source, target, column, share, own_sem in both:
        share.every(
            lambda there, target=target, share=share: share.got(
                target.at[aligned(2 * there + other, rows), :], there
            )
        )
    key_t[...] = jnp.transpose(key_all[...])
    value_t[...] = jnp.transpose(value_all[...])
    base_move.wait_recv()

    documents = meta_all[0:1, :]
    cuts = [
        jnp.sum(jnp.where(documents < number, 1, 0), axis=1, keepdims=True) for number in (1, 2, 3)
    ]

    def slots_of(there, all_ref):
        slot_row = meta_all[1:2, aligned(there, block)]
        low = jnp.concatenate([all_ref[2 * there], all_ref[2 * there + 1]], axis=1)
        return slot_row, spread_slots(slot_row, low, picks)

    def blocks_of(there):
        return (there * block + block - 1) // key_block + 1

    def forward_step(there):
        place = aligned(there, block)
        _, low_spread = slots_of(there, low_all)
        lifted = dot(up_t[...], low_spread)
        queries = (base_all[place, :].astype(F32) + jnp.transpose(lifted)).astype(BF16)
        queries_all[place, :] = queries
        position = there * block + lax.broadcasted_iota(jnp.int32, (1, block), 1)
        start = jnp.zeros((1, block), jnp.int32)
        for cut in cuts:
            start = jnp.where(position >= cut, cut, start)

        def score_step(index, peak):
            keys = aligned(index, key_block)
            logits = dot_nt(key_all[keys, :], queries) * (SCALE * LOG2E)
            key_position = index * key_block + lax.broadcasted_iota(
                jnp.int32, (key_block, block), 0
            )
            logits = jnp.where(
                (key_position <= position) & (key_position >= start), logits, MASKED
            )
            scores[keys, :] = logits
            return jnp.maximum(peak, jnp.max(logits.reshape(-1, 8, block), axis=0))

        peak8 = lax.fori_loop(
            0, blocks_of(there), score_step, jnp.full((8, block), MASKED, F32)
        )
        peak = jnp.max(peak8, axis=0, keepdims=True)

        def weight_step(index, state):
            total, mixed = state
            keys = aligned(index, key_block)
            weight = jnp.exp2(scores[keys, :] - peak)
            weight_low = weight.astype(BF16)
            weights[there, keys, :] = weight_low
            total = total + jnp.sum(weight.reshape(-1, 8, block), axis=0)
            return total, mixed + dot(value_t[:, keys], weight_low)

        total8, mixed = lax.fori_loop(
            0,
            blocks_of(there),
            weight_step,
            (jnp.zeros((8, block), F32), jnp.zeros((HEAD, block), F32)),
        )
        inverse = 1.0 / jnp.sum(total8, axis=0, keepdims=True)
        stats[there] = jnp.broadcast_to(inverse, (8, block))
        out_all[place, :] = jnp.transpose((mixed * inverse).astype(BF16))
        for part in range(2):
            dest = 2 * there + part

            @pl.when(dest != me)
            def _():
                out_move.copy(dest, me).start()

    gradient_move.start()
    loop(0, planes, lambda step: forward_step(columns[0].away(step)))
    out_move.own().start()
    gradient_move.wait_recv()
    up_sum[...] = jnp.zeros_like(up_sum)

    def backward_step(there):
        place = aligned(there, block)
        slot_row, low_spread = slots_of(there, low_all)
        gradient_t = jnp.transpose(gradient_all[place, :]).astype(F32) * stats[there, 0:1, :]
        out_t = jnp.transpose(out_all[place, :]).astype(F32)
        delta = jnp.sum(gradient_t * out_t, axis=0, keepdims=True)
        gradient_low = jnp.transpose(gradient_t.astype(BF16))
        gradient_all[place, :] = gradient_low

        def back_step(index, query_sum):
            keys = aligned(index, key_block)
            dprobs = dot_nt(value_all[keys, :], gradient_low)
            dscores = (weights[there, keys, :].astype(F32) * (dprobs - delta)).astype(BF16)
            dscores_all[there, keys, :] = dscores
            return query_sum + dot(key_t[:, keys], dscores)

        query_sum = lax.fori_loop(
            0, blocks_of(there), back_step, jnp.zeros((HEAD, block), F32)
        )
        query_grad = (query_sum * SCALE).astype(BF16)
        each = dot(up_picked[...], query_grad)
        low = fold_slots(slot_row, each, picks).astype(BF16)
        deal(low, there, grad_part, grad_move)
        up_sum[...] += dot_nt(low_spread, query_grad)

    loop(0, planes, lambda step: backward_step(columns[0].away(step)))

    tenants = [adapters[own_seq, pick] for pick in range(picks)]

    def build_table(total_ref, table_ref):
        def table_step(tenant):
            total = jnp.zeros((RANK, total_ref.shape[1]), F32)
            for pick in range(picks):
                here = (tenants[pick] == tenant).astype(F32)
                total = total + total_ref[pick * RANK : (pick + 1) * RANK, :] * here
            table_ref[tenant] = total.astype(BF16)

        loop(0, seq_count, table_step)

    build_table(up_sum, up_table)
    up_back.start()

    key_x, value_x, key_z, value_z = columns[4:8]

    lag = planes

    def key_step(shift):
        there = key_x.away(shift)
        place = aligned(there, block)

        def query_step(index, state):
            keys_acc, values_acc = state
            from_rows = aligned(index, block)
            values_acc = values_acc + dot(weights[index, place, :], gradient_all[from_rows, :])
            keys_acc = keys_acc + dot(dscores_all[index, place, :], queries_all[from_rows, :])
            return keys_acc, values_acc

        zero = jnp.zeros((block, HEAD), F32)
        keys_acc, values_acc = lax.fori_loop(there, planes, query_step, (zero, zero))
        keys_low = (keys_acc * SCALE).astype(BF16)
        values_low = values_acc.astype(BF16)
        for part in range(2):
            key_out[there, part] = keys_low[part * rows : (part + 1) * rows]
            value_out[there, part] = values_low[part * rows : (part + 1) * rows]
        key_x.to_twin(key_out.at[there, other], key_pair.at[there], there)
        value_x.to_twin(value_out.at[there, other], value_pair.at[there], there)

        @pl.when(shift >= lag)
        def _():
            pass_on(key_x.away(shift - lag))

    def pass_on(there):
        for pair_column, column, part, pair, total, recv_ref in (
            (key_x, key_z, key_out, key_pair, key_mid, key_recv),
            (value_x, value_z, value_out, value_pair, value_mid, value_recv),
        ):
            pair_column.got(pair.at[there], there)
            total[there] = (
                part[there, side].astype(F32) + pair[there].astype(F32)
            ).astype(BF16)

            @pl.when(there != plane)
            def _():
                column.to_plane(total.at[there], recv_ref.at[plane], there)

    first_cut, second_cut = planes // 4, planes
    loop(0, first_cut, key_step)
    collect(grad_part, grad_recv, grad_all, grad_move, grad_gather)
    loop(first_cut, second_cut, key_step)
    grad_gather.wait_recv()
    down_sum[...] = jnp.zeros_like(down_sum)

    def down_step(there):
        _, spread = slots_of(there, grad_all)
        down_sum[...] += dot(spread, tokens_all[aligned(there, block), :])

    loop(0, planes, down_step)
    build_table(down_sum, down_table)
    down_back.start()
    loop(second_cut, planes, key_step)
    loop(planes - lag, planes, lambda shift: pass_on(key_x.away(shift)))

    members = group // 2
    for column, total, recv_ref, grad in (
        (key_z, key_mid, key_recv, key_grad),
        (value_z, value_mid, value_recv, value_grad),
    ):
        recv_ref[plane] = total[plane]
        column.others(
            lambda there, column=column, recv_ref=recv_ref: column.got(recv_ref.at[there], there)
        )
        for head in range(planes // members):
            acc = recv_ref[head * members].astype(F32)
            for member in range(1, members):
                acc = acc + recv_ref[head * members + member].astype(F32)
            grad[:, head * HEAD : (head + 1) * HEAD] = acc

    def add_up(recv_ref, grad):
        grad[...] = lax.fori_loop(
            0,
            seq_count,
            lambda index, acc: acc + recv_ref[index].astype(F32),
            jnp.zeros(grad.shape, F32),
        )

    up_back.wait_recv()
    add_up(up_recv, up_grad)
    out_move.wait_recv()
    down_back.wait_recv()
    add_up(down_recv, down_grad)

    for move in (
        x_move,
        meta_move,
        base_move,
        gradient_move,
        out_move,
        down_move,
        up_move,
        up_back,
        down_back,
        low_move,
        low_gather,
        grad_move,
        grad_gather,
    ):
        move.wait_send()
    for source, target, column, share, _ in both:
        column.others(
            lambda there, source=source, column=column: column.sent(
                source.at[:, head_of(there)], there
            )
        )
        share.every(
            lambda there, target=target, share=share: share.sent(
                target.at[aligned(2 * there + side, rows), :], there
            )
        )
    for pair_column, part in (
        (key_x, key_out),
        (value_x, value_out),
    ):
        pair_column.every(
            lambda there, pair_column=pair_column, part=part: pair_column.sent(
                part.at[there, other], there
            )
        )
    for column, total in (
        (key_z, key_mid),
        (value_z, value_mid),
    ):
        column.others(
            lambda there, column=column, total=total: column.sent(total.at[there], there)
        )


def hand_over_kernel(*refs):
    for source, target in zip(refs[:5], refs[5:]):
        target[...] = source[...]


def vmem():
    return pl.BlockSpec(memory_space=pltpu.VMEM)


def hbm():
    return pl.BlockSpec(memory_space=pltpu.HBM)


def smem():
    return pl.BlockSpec(memory_space=pltpu.SMEM)


def per_device(
    normed_hidden_input,
    frozen_query_base,
    key_head_states,
    value_head_states,
    document_numbers,
    tenant_block_entry,
    sequence_adapter_list,
    adapter_down_weight,
    adapter_up_weight,
    output_gradient,
):
    ctx_count = lax.axis_size("ctx")
    seq_count = lax.axis_size("seq")
    planes = ctx_count // 2
    rows = normed_hidden_input.shape[1]
    length = rows * ctx_count
    width = adapter_down_weight.shape[2]
    picks = sequence_adapter_list.shape[1]
    key_heads = key_head_states.shape[2] // HEAD
    group = ctx_count // key_heads
    stacked = picks * RANK
    token_slots = jnp.repeat(tenant_block_entry, TB, axis=1)
    meta = jnp.pad(jnp.concatenate([document_numbers, token_slots], axis=0), ((0, 6), (0, 0)))

    def shape(dims, dtype=BF16):
        return jax.ShapeDtypeStruct(dims, dtype)

    head_rows = pltpu.VMEM((length, HEAD), BF16)
    low_blocks = pltpu.VMEM((ctx_count, RANK, rows), BF16)
    key_plane = pltpu.VMEM((planes, rows, HEAD), BF16)
    key_buffers = [pltpu.VMEM((planes, 2, rows, HEAD), BF16), key_plane, key_plane, key_plane]
    attention, key_grad, value_grad, down_grad, up_grad = pl.pallas_call(
        functools.partial(fused_kernel, ctx_count, seq_count, group),
        name="attention_layer",
        out_shape=(
            shape((rows, ctx_count * HEAD)),
            shape((rows, key_heads * HEAD), F32),
            shape((rows, key_heads * HEAD), F32),
            shape((RANK, width), F32),
            shape((RANK, HEAD), F32),
        ),
        in_specs=[hbm()] * 8 + [smem()],
        out_specs=(hbm(), vmem(), vmem(), vmem(), vmem()),
        scratch_shapes=[
            pltpu.VMEM((length, width), BF16),
            head_rows,
            head_rows,
            head_rows,
            head_rows,
            pltpu.VMEM((8, length), jnp.int32),
            pltpu.VMEM((seq_count, RANK, width), BF16),
            pltpu.VMEM((seq_count, RANK, HEAD), BF16),
            pltpu.VMEM((stacked, width), BF16),
            pltpu.VMEM((stacked, HEAD), BF16),
            pltpu.VMEM((HEAD, stacked), BF16),
            *[low_blocks] * 6,
            head_rows,
            head_rows,
            pltpu.VMEM((planes, length, 2 * rows), BF16),
            pltpu.VMEM((planes, length, 2 * rows), BF16),
            pltpu.VMEM((length, 2 * rows), F32),
            pltpu.VMEM((planes, 8, 2 * rows), F32),
            pltpu.VMEM((HEAD, length), BF16),
            pltpu.VMEM((HEAD, length), BF16),
            *key_buffers,
            *key_buffers,
            pltpu.VMEM((stacked, HEAD), F32),
            pltpu.VMEM((seq_count, RANK, HEAD), BF16),
            pltpu.VMEM((seq_count, RANK, HEAD), BF16),
            pltpu.VMEM((stacked, width), F32),
            pltpu.VMEM((seq_count, RANK, width), BF16),
            pltpu.VMEM((seq_count, RANK, width), BF16),
            pltpu.SemaphoreType.DMA((9, ctx_count)),
            pltpu.SemaphoreType.DMA((9, ctx_count)),
            pltpu.SemaphoreType.DMA((8, planes)),
            pltpu.SemaphoreType.DMA((8, planes)),
            pltpu.SemaphoreType.DMA((4, seq_count)),
            pltpu.SemaphoreType.DMA((4, seq_count)),
            pltpu.SemaphoreType.DMA((11,)),
        ],
        compiler_params=pltpu.CompilerParams(
            collective_id=0, has_side_effects=True, vmem_limit_bytes=56 << 20
        ),
    )(
        normed_hidden_input[0],
        frozen_query_base[0],
        key_head_states[0],
        value_head_states[0],
        output_gradient[0],
        meta,
        adapter_down_weight[0],
        adapter_up_weight[0],
        sequence_adapter_list,
    )
    attention, key_grad, value_grad, down_grad, up_grad = pl.pallas_call(
        hand_over_kernel,
        name="hand_over",
        out_shape=tuple(
            shape(array.shape, array.dtype)
            for array in (attention, key_grad, value_grad, down_grad, up_grad)
        ),
        in_specs=[vmem()] * 5,
        out_specs=(vmem(),) * 5,
    )(attention, key_grad, value_grad, down_grad, up_grad)
    return (
        attention[None],
        key_grad[None],
        value_grad[None],
        down_grad[None],
        up_grad[None],
    )


def solution(mesh):
    in_specs = (
        P("seq", "ctx", None),
        P("seq", "ctx", None),
        P("seq", "ctx", None),
        P("seq", "ctx", None),
        P("seq", "ctx"),
        P("seq", "ctx"),
        P(),
        P("seq", None, "ctx"),
        P("seq", None, "ctx"),
        P("seq", "ctx", None),
    )
    out_specs = (
        P("seq", "ctx", None),
        P("seq", "ctx", None),
        P("seq", "ctx", None),
        P("seq", None, "ctx"),
        P("seq", None, "ctx"),
    )
    return jax.shard_map(
        per_device, mesh=mesh, in_specs=in_specs, out_specs=out_specs, check_vma=False
    )
```

```python
import functools
import math

import jax
import jax.numpy as jnp
from jax import lax
from jax.experimental import pallas as pl
from jax.experimental.pallas import tpu as pltpu
from jax.sharding import PartitionSpec as P

MESH = pl.DeviceIdType.MESH
BF16 = jnp.bfloat16
F32 = jnp.float32
HEAD = 128
RANK = 64
TB = 32
KEY_BLOCK = 1024
MASKED = -1e30
SCALE = 1.0 / math.sqrt(HEAD)
LOG2E = math.log2(math.e)


def dot(a, b):
    return lax.dot_general(a, b, (((1,), (0,)), ((), ())), preferred_element_type=F32)


def dot_nt(a, b):
    return lax.dot_general(a, b, (((1,), (1,)), ((), ())), preferred_element_type=F32)


def aligned(index, size):
    return pl.ds(pl.multiple_of(index * size, size), size)


def push(source, target, send, recv, dest):
    return pltpu.make_async_remote_copy(
        src_ref=source,
        dst_ref=target,
        send_sem=send,
        recv_sem=recv,
        device_id=dest,
        device_id_type=MESH,
    )


def loop(low, high, body):
    def step(index, carry):
        body(index)
        return carry

    lax.fori_loop(low, high, step, 0)


class Exchange:
    def __init__(self, axis, count, me, source, target, send, recv, local):
        self.axis, self.count, self.me = axis, count, me
        self.source, self.target = source, target
        self.send, self.recv, self.local = send, recv, local

    def copy(self, peer, place):
        return push(
            self.source(peer),
            self.target(place),
            self.send.at[peer],
            self.recv.at[place],
            {self.axis: peer},
        )

    def own(self):
        return pltpu.make_async_copy(self.source(self.me), self.target(self.me), self.local)

    def each(self, body):
        loop(1, self.count, lambda shift: body(lax.rem(self.me + shift, self.count)))

    def start(self):
        self.each(lambda peer: self.copy(peer, self.me).start())
        if self.local is not None:
            self.own().start()

    def wait_from(self, place):
        self.copy(place, place).wait_recv()

    def wait_recv(self):
        loop(
            1,
            self.count,
            lambda shift: self.wait_from(lax.rem(self.me + self.count - shift, self.count)),
        )
        if self.local is not None:
            self.own().wait()

    def wait_send(self):
        self.each(lambda peer: self.copy(peer, self.me).wait_send())


class Column:
    def __init__(self, planes, plane, side, send, recv):
        self.planes, self.plane, self.side = planes, plane, side
        self.send, self.recv = send, recv

    def to_plane(self, source, target, there):
        dest = {"ctx": there * 2 + self.side}
        push(source, target, self.send.at[there], self.recv.at[self.plane], dest).start()

    def to_twin(self, source, target, index):
        dest = {"ctx": self.plane * 2 + 1 - self.side}
        push(source, target, self.send.at[index], self.recv.at[index], dest).start()

    def got(self, target, index):
        dest = {"ctx": self.plane * 2 + 1 - self.side}
        push(target, target, self.send.at[index], self.recv.at[index], dest).wait_recv()

    def sent(self, source, index):
        dest = {"ctx": self.plane * 2 + 1 - self.side}
        push(source, source, self.send.at[index], self.recv.at[index], dest).wait_send()

    def others(self, body):
        loop(1, self.planes, lambda shift: body(lax.rem(self.plane + shift, self.planes)))

    def every(self, body):
        loop(0, self.planes, lambda shift: body(lax.rem(self.plane + shift, self.planes)))

    def away(self, step):
        left = self.planes - step
        shift = jnp.where(lax.rem(left, 2) == 0, left // 2, -(left // 2))
        return lax.rem(self.plane + self.planes + shift, self.planes)

    def arrivals(self, body, first=0):
        loop(
            first,
            self.planes,
            lambda shift: body(lax.rem(self.plane + self.planes - shift, self.planes)),
        )


def meet(me_ctx, ctx_count, me_seq, seq_count):
    barrier = pltpu.get_barrier_semaphore()

    def greet(axis, me, count):
        def step(shift):
            pl.semaphore_signal(
                barrier,
                inc=1,
                device_id={axis: lax.rem(me + shift, count)},
                device_id_type=MESH,
            )

        loop(1, count, step)

    greet("ctx", me_ctx, ctx_count)
    greet("seq", me_seq, seq_count)
    pl.semaphore_wait(barrier, ctx_count + seq_count - 2)


def spread_slots(slot_row, low, picks):
    zero = jnp.zeros_like(low)
    return jnp.concatenate(
        [jnp.where(slot_row == pick, low, zero) for pick in range(picks)], axis=0
    )


def fold_slots(slot_row, each, picks):
    total = jnp.zeros((RANK, each.shape[1]), F32)
    for pick in range(picks):
        part = each[pick * RANK : (pick + 1) * RANK]
        total = total + jnp.where(slot_row == pick, part, 0.0)
    return total


def fused_kernel(
    ctx_count,
    seq_count,
    group,
    tokens,
    base,
    key,
    value,
    gradient,
    meta,
    down,
    up,
    adapters,
    attention,
    key_grad,
    value_grad,
    down_grad,
    up_grad,
    tokens_all,
    base_all,
    key_all,
    value_all,
    gradient_all,
    meta_all,
    down_tenants,
    up_tenants,
    down_picked,
    up_picked,
    up_t,
    low_part,
    low_recv,
    low_all,
    grad_part,
    grad_recv,
    grad_all,
    queries_all,
    out_all,
    weights,
    dscores_all,
    scores,
    stats,
    key_t,
    value_t,
    key_out,
    key_pair,
    key_mid,
    key_recv,
    value_out,
    value_pair,
    value_mid,
    value_recv,
    up_sum,
    up_table,
    up_recv,
    down_sum,
    down_table,
    down_recv,
    send,
    recv,
    send_z,
    recv_z,
    send_seq,
    recv_seq,
    local,
):
    me = lax.axis_index("ctx")
    own_seq = lax.axis_index("seq")
    planes = ctx_count // 2
    plane, side = me // 2, lax.rem(me, 2)
    other = 1 - side
    rows = tokens.shape[0]
    block = 2 * rows
    length = tokens_all.shape[0]
    width = tokens_all.shape[1]
    picks = adapters.shape[1]
    key_block = min(KEY_BLOCK, length)

    def over_ctx(slot, source, target, has_own=True):
        return Exchange(
            "ctx",
            ctx_count,
            me,
            source,
            target,
            send.at[slot],
            recv.at[slot],
            local.at[slot] if has_own else None,
        )

    def over_seq(slot, source, target):
        return Exchange(
            "seq",
            seq_count,
            own_seq,
            source,
            target,
            send_seq.at[slot],
            recv_seq.at[slot],
            local.at[5 + slot],
        )

    columns = [
        Column(planes, plane, side, send_z.at[slot], recv_z.at[slot])
        for slot in range(send_z.shape[0])
    ]
    x_move = over_ctx(
        0,
        lambda peer: tokens.at[:, aligned(peer, width)],
        lambda place: tokens_all.at[aligned(place, rows), :],
    )
    meta_move = over_ctx(
        1, lambda peer: meta, lambda place: meta_all.at[:, aligned(place, rows)]
    )
    base_move = over_ctx(
        2,
        lambda peer: base.at[:, aligned(peer, HEAD)],
        lambda place: base_all.at[aligned(place, rows), :],
    )
    gradient_move = over_ctx(
        3,
        lambda peer: gradient.at[:, aligned(peer, HEAD)],
        lambda place: gradient_all.at[aligned(place, rows), :],
    )
    out_move = over_ctx(
        4,
        lambda peer: out_all.at[aligned(peer, rows), :],
        lambda place: attention.at[:, aligned(place, HEAD)],
    )
    grad_move = over_ctx(
        5, lambda peer: grad_part.at[peer], lambda place: grad_recv.at[place], has_own=False
    )
    grad_gather = over_ctx(
        6, lambda peer: grad_all.at[me], lambda place: grad_all.at[place], has_own=False
    )
    low_move = over_ctx(
        7, lambda peer: low_part.at[peer], lambda place: low_recv.at[place], has_own=False
    )
    low_gather = over_ctx(
        8, lambda peer: low_all.at[me], lambda place: low_all.at[place], has_own=False
    )
    down_move = over_seq(0, lambda peer: down, lambda place: down_tenants.at[place])
    up_move = over_seq(1, lambda peer: up, lambda place: up_tenants.at[place])
    up_back = over_seq(2, lambda peer: up_table.at[peer], lambda place: up_recv.at[place])
    down_back = over_seq(3, lambda peer: down_table.at[peer], lambda place: down_recv.at[place])
    both = (
        (key, key_all, columns[0], columns[1], local.at[9]),
        (value, value_all, columns[2], columns[3], local.at[10]),
    )

    meet(me, ctx_count, own_seq, seq_count)

    def head_of(there):
        return aligned((2 * there) // group, HEAD)

    def own_rows():
        return aligned(me, rows)

    def key_send():
        for source, target, column, _, own_sem in both:
            column.others(
                lambda there, source=source, target=target, column=column: column.to_plane(
                    source.at[:, head_of(there)], target.at[own_rows(), :], there
                )
            )
            pltpu.make_async_copy(
                source.at[:, head_of(plane)], target.at[own_rows(), :], own_sem
            ).start()

    def key_forward():
        for source, target, column, share, own_sem in both:
            pltpu.make_async_copy(
                source.at[:, head_of(plane)], target.at[own_rows(), :], own_sem
            ).wait()

            def forward(there, target=target, column=column, share=share):
                place = target.at[aligned(2 * there + side, rows), :]

                @pl.when(there != plane)
                def _():
                    column.got(place, there)

                share.to_twin(place, place, there)

            column.arrivals(forward)

    down_move.start()
    meta_move.start()
    x_move.start()
    up_move.start()
    base_move.start()

    meta_move.wait_recv()
    down_move.wait_recv()
    for pick in range(picks):
        down_picked[pick * RANK : (pick + 1) * RANK, :] = down_tenants[adapters[own_seq, pick]]

    x_move.own().wait()

    def deal(low, there, part_ref, move):
        for part in range(2):
            dest = 2 * there + part
            part_ref[dest] = low[:, part * rows : (part + 1) * rows]

            @pl.when(dest != me)
            def _():
                move.copy(dest, me).start()

    def collect(part_ref, recv_ref, all_ref, move, gather):
        recv_ref[me] = part_ref[me]
        move.wait_recv()
        all_ref[me] = lax.fori_loop(
            0,
            ctx_count,
            lambda place, acc: acc + recv_ref[place].astype(F32),
            jnp.zeros((RANK, rows), F32),
        ).astype(BF16)
        gather.start()

    def low_step(there):
        for part in range(2):
            place = 2 * there + part

            @pl.when(place != me)
            def _():
                x_move.wait_from(place)

        cols = aligned(there, block)
        each = dot_nt(down_picked[...], tokens_all[cols, :])
        low = fold_slots(meta_all[1:2, cols], each, picks).astype(BF16)
        deal(low, there, low_part, low_move)

    columns[0].arrivals(low_step)
    key_send()

    collect(low_part, low_recv, low_all, low_move, low_gather)
    key_forward()
    low_gather.wait_recv()
    up_move.wait_recv()
    for pick in range(picks):
        up_picked[pick * RANK : (pick + 1) * RANK, :] = up_tenants[adapters[own_seq, pick]]
    up_t[...] = jnp.transpose(up_picked[...])
    for source, target, column, share, own_sem in both:
        share.every(
            lambda there, target=target, share=share: share.got(
                target.at[aligned(2 * there + other, rows), :], there
            )
        )
    key_t[...] = jnp.transpose(key_all[...])
    value_t[...] = jnp.transpose(value_all[...])
    base_move.wait_recv()

    documents = meta_all[0:1, :]
    cuts = [
        jnp.sum(jnp.where(documents < number, 1, 0), axis=1, keepdims=True) for number in (1, 2, 3)
    ]

    def slots_of(there, all_ref):
        slot_row = meta_all[1:2, aligned(there, block)]
        low = jnp.concatenate([all_ref[2 * there], all_ref[2 * there + 1]], axis=1)
        return slot_row, spread_slots(slot_row, low, picks)

    def blocks_of(there):
        return (there * block + block - 1) // key_block + 1

    def forward_step(there):
        place = aligned(there, block)
        _, low_spread = slots_of(there, low_all)
        lifted = dot(up_t[...], low_spread)
        queries = (base_all[place, :].astype(F32) + jnp.transpose(lifted)).astype(BF16)
        queries_all[place, :] = queries
        position = there * block + lax.broadcasted_iota(jnp.int32, (1, block), 1)
        start = jnp.zeros((1, block), jnp.int32)
        for cut in cuts:
            start = jnp.where(position >= cut, cut, start)

        def score_step(index, peak):
            keys = aligned(index, key_block)
            logits = dot_nt(key_all[keys, :], queries) * (SCALE * LOG2E)
            key_position = index * key_block + lax.broadcasted_iota(
                jnp.int32, (key_block, block), 0
            )
            logits = jnp.where(
                (key_position <= position) & (key_position >= start), logits, MASKED
            )
            scores[keys, :] = logits
            return jnp.maximum(peak, jnp.max(logits.reshape(-1, 8, block), axis=0))

        peak8 = lax.fori_loop(
            0, blocks_of(there), score_step, jnp.full((8, block), MASKED, F32)
        )
        peak = jnp.max(peak8, axis=0, keepdims=True)

        def weight_step(index, state):
            total, mixed = state
            keys = aligned(index, key_block)
            weight = jnp.exp2(scores[keys, :] - peak)
            weight_low = weight.astype(BF16)
            weights[there, keys, :] = weight_low
            total = total + jnp.sum(weight.reshape(-1, 8, block), axis=0)
            return total, mixed + dot(value_t[:, keys], weight_low)

        total8, mixed = lax.fori_loop(
            0,
            blocks_of(there),
            weight_step,
            (jnp.zeros((8, block), F32), jnp.zeros((HEAD, block), F32)),
        )
        inverse = 1.0 / jnp.sum(total8, axis=0, keepdims=True)
        stats[there] = jnp.broadcast_to(inverse, (8, block))
        out_all[place, :] = jnp.transpose((mixed * inverse).astype(BF16))
        for part in range(2):
            dest = 2 * there + part

            @pl.when(dest != me)
            def _():
                out_move.copy(dest, me).start()

    gradient_move.start()
    loop(0, planes, lambda step: forward_step(columns[0].away(step)))
    out_move.own().start()
    gradient_move.wait_recv()
    up_sum[...] = jnp.zeros_like(up_sum)

    def backward_step(there):
        place = aligned(there, block)
        slot_row, low_spread = slots_of(there, low_all)
        gradient_t = jnp.transpose(gradient_all[place, :]).astype(F32) * stats[there, 0:1, :]
        out_t = jnp.transpose(out_all[place, :]).astype(F32)
        delta = jnp.sum(gradient_t * out_t, axis=0, keepdims=True)
        gradient_low = jnp.transpose(gradient_t.astype(BF16))
        gradient_all[place, :] = gradient_low

        def back_step(index, query_sum):
            keys = aligned(index, key_block)
            dprobs = dot_nt(value_all[keys, :], gradient_low)
            dscores = (weights[there, keys, :].astype(F32) * (dprobs - delta)).astype(BF16)
            dscores_all[there, keys, :] = dscores
            return query_sum + dot(key_t[:, keys], dscores)

        query_sum = lax.fori_loop(
            0, blocks_of(there), back_step, jnp.zeros((HEAD, block), F32)
        )
        query_grad = (query_sum * SCALE).astype(BF16)
        each = dot(up_picked[...], query_grad)
        low = fold_slots(slot_row, each, picks).astype(BF16)
        deal(low, there, grad_part, grad_move)
        up_sum[...] += dot_nt(low_spread, query_grad)

    loop(0, planes, lambda step: backward_step(columns[0].away(step)))

    tenants = [adapters[own_seq, pick] for pick in range(picks)]

    def build_table(total_ref, table_ref):
        def table_step(tenant):
            total = jnp.zeros((RANK, total_ref.shape[1]), F32)
            for pick in range(picks):
                here = (tenants[pick] == tenant).astype(F32)
                total = total + total_ref[pick * RANK : (pick + 1) * RANK, :] * here
            table_ref[tenant] = total.astype(BF16)

        loop(0, seq_count, table_step)

    build_table(up_sum, up_table)
    up_back.start()

    key_x, value_x, key_z, value_z = columns[4:8]

    lag = planes

    def key_step(shift):
        there = key_x.away(shift)
        place = aligned(there, block)

        def query_step(index, state):
            keys_acc, values_acc = state
            from_rows = aligned(index, block)
            values_acc = values_acc + dot(weights[index, place, :], gradient_all[from_rows, :])
            keys_acc = keys_acc + dot(dscores_all[index, place, :], queries_all[from_rows, :])
            return keys_acc, values_acc

        zero = jnp.zeros((block, HEAD), F32)
        keys_acc, values_acc = lax.fori_loop(there, planes, query_step, (zero, zero))
        keys_low = (keys_acc * SCALE).astype(BF16)
        values_low = values_acc.astype(BF16)
        for part in range(2):
            key_out[there, part] = keys_low[part * rows : (part + 1) * rows]
            value_out[there, part] = values_low[part * rows : (part + 1) * rows]
        key_x.to_twin(key_out.at[there, other], key_pair.at[there], there)
        value_x.to_twin(value_out.at[there, other], value_pair.at[there], there)

        @pl.when(shift >= lag)
        def _():
            pass_on(key_x.away(shift - lag))

    def pass_on(there):
        for pair_column, column, part, pair, total, recv_ref in (
            (key_x, key_z, key_out, key_pair, key_mid, key_recv),
            (value_x, value_z, value_out, value_pair, value_mid, value_recv),
        ):
            pair_column.got(pair.at[there], there)
            total[there] = (
                part[there, side].astype(F32) + pair[there].astype(F32)
            ).astype(BF16)

            @pl.when(there != plane)
            def _():
                column.to_plane(total.at[there], recv_ref.at[plane], there)

    first_cut, second_cut = planes // 4, planes
    loop(0, first_cut, key_step)
    collect(grad_part, grad_recv, grad_all, grad_move, grad_gather)
    loop(first_cut, second_cut, key_step)
    grad_gather.wait_recv()
    down_sum[...] = jnp.zeros_like(down_sum)

    def down_step(there):
        _, spread = slots_of(there, grad_all)
        down_sum[...] += dot(spread, tokens_all[aligned(there, block), :])

    loop(0, planes, down_step)
    build_table(down_sum, down_table)
    down_back.start()
    loop(second_cut, planes, key_step)
    loop(planes - lag, planes, lambda shift: pass_on(key_x.away(shift)))

    members = group // 2
    for column, total, recv_ref, grad in (
        (key_z, key_mid, key_recv, key_grad),
        (value_z, value_mid, value_recv, value_grad),
    ):
        recv_ref[plane] = total[plane]
        column.others(
            lambda there, column=column, recv_ref=recv_ref: column.got(recv_ref.at[there], there)
        )
        for head in range(planes // members):
            acc = recv_ref[head * members].astype(F32)
            for member in range(1, members):
                acc = acc + recv_ref[head * members + member].astype(F32)
            grad[:, head * HEAD : (head + 1) * HEAD] = acc

    def add_up(recv_ref, grad):
        grad[...] = lax.fori_loop(
            0,
            seq_count,
            lambda index, acc: acc + recv_ref[index].astype(F32),
            jnp.zeros(grad.shape, F32),
        )

    up_back.wait_recv()
    add_up(up_recv, up_grad)
    out_move.wait_recv()
    down_back.wait_recv()
    add_up(down_recv, down_grad)

    for move in (
        x_move,
        meta_move,
        base_move,
        gradient_move,
        out_move,
        down_move,
        up_move,
        up_back,
        down_back,
        low_move,
        low_gather,
        grad_move,
        grad_gather,
    ):
        move.wait_send()
    for source, target, column, share, _ in both:
        column.others(
            lambda there, source=source, column=column: column.sent(
                source.at[:, head_of(there)], there
            )
        )
        share.every(
            lambda there, target=target, share=share: share.sent(
                target.at[aligned(2 * there + side, rows), :], there
            )
        )
    for pair_column, part in (
        (key_x, key_out),
        (value_x, value_out),
    ):
        pair_column.every(
            lambda there, pair_column=pair_column, part=part: pair_column.sent(
                part.at[there, other], there
            )
        )
    for column, total in (
        (key_z, key_mid),
        (value_z, value_mid),
    ):
        column.others(
            lambda there, column=column, total=total: column.sent(total.at[there], there)
        )


def hand_over_kernel(*refs):
    for source, target in zip(refs[:5], refs[5:]):
        target[...] = source[...]


def vmem():
    return pl.BlockSpec(memory_space=pltpu.VMEM)


def hbm():
    return pl.BlockSpec(memory_space=pltpu.HBM)


def smem():
    return pl.BlockSpec(memory_space=pltpu.SMEM)


def per_device(
    normed_hidden_input,
    frozen_query_base,
    key_head_states,
    value_head_states,
    document_numbers,
    tenant_block_entry,
    sequence_adapter_list,
    adapter_down_weight,
    adapter_up_weight,
    output_gradient,
):
    ctx_count = lax.axis_size("ctx")
    seq_count = lax.axis_size("seq")
    planes = ctx_count // 2
    rows = normed_hidden_input.shape[1]
    length = rows * ctx_count
    width = adapter_down_weight.shape[2]
    picks = sequence_adapter_list.shape[1]
    key_heads = key_head_states.shape[2] // HEAD
    group = ctx_count // key_heads
    stacked = picks * RANK
    token_slots = jnp.repeat(tenant_block_entry, TB, axis=1)
    meta = jnp.pad(jnp.concatenate([document_numbers, token_slots], axis=0), ((0, 6), (0, 0)))

    def shape(dims, dtype=BF16):
        return jax.ShapeDtypeStruct(dims, dtype)

    head_rows = pltpu.VMEM((length, HEAD), BF16)
    low_blocks = pltpu.VMEM((ctx_count, RANK, rows), BF16)
    key_plane = pltpu.VMEM((planes, rows, HEAD), BF16)
    key_buffers = [pltpu.VMEM((planes, 2, rows, HEAD), BF16), key_plane, key_plane, key_plane]
    attention, key_grad, value_grad, down_grad, up_grad = pl.pallas_call(
        functools.partial(fused_kernel, ctx_count, seq_count, group),
        name="attention_layer",
        out_shape=(
            shape((rows, ctx_count * HEAD)),
            shape((rows, key_heads * HEAD), F32),
            shape((rows, key_heads * HEAD), F32),
            shape((RANK, width), F32),
            shape((RANK, HEAD), F32),
        ),
        in_specs=[hbm()] * 8 + [smem()],
        out_specs=(hbm(), vmem(), vmem(), vmem(), vmem()),
        scratch_shapes=[
            pltpu.VMEM((length, width), BF16),
            head_rows,
            head_rows,
            head_rows,
            head_rows,
            pltpu.VMEM((8, length), jnp.int32),
            pltpu.VMEM((seq_count, RANK, width), BF16),
            pltpu.VMEM((seq_count, RANK, HEAD), BF16),
            pltpu.VMEM((stacked, width), BF16),
            pltpu.VMEM((stacked, HEAD), BF16),
            pltpu.VMEM((HEAD, stacked), BF16),
            *[low_blocks] * 6,
            head_rows,
            head_rows,
            pltpu.VMEM((planes, length, 2 * rows), BF16),
            pltpu.VMEM((planes, length, 2 * rows), BF16),
            pltpu.VMEM((length, 2 * rows), F32),
            pltpu.VMEM((planes, 8, 2 * rows), F32),
            pltpu.VMEM((HEAD, length), BF16),
            pltpu.VMEM((HEAD, length), BF16),
            *key_buffers,
            *key_buffers,
            pltpu.VMEM((stacked, HEAD), F32),
            pltpu.VMEM((seq_count, RANK, HEAD), BF16),
            pltpu.VMEM((seq_count, RANK, HEAD), BF16),
            pltpu.VMEM((stacked, width), F32),
            pltpu.VMEM((seq_count, RANK, width), BF16),
            pltpu.VMEM((seq_count, RANK, width), BF16),
            pltpu.SemaphoreType.DMA((9, ctx_count)),
            pltpu.SemaphoreType.DMA((9, ctx_count)),
            pltpu.SemaphoreType.DMA((8, planes)),
            pltpu.SemaphoreType.DMA((8, planes)),
            pltpu.SemaphoreType.DMA((4, seq_count)),
            pltpu.SemaphoreType.DMA((4, seq_count)),
            pltpu.SemaphoreType.DMA((11,)),
        ],
        compiler_params=pltpu.CompilerParams(
            collective_id=0, has_side_effects=True, vmem_limit_bytes=56 << 20
        ),
    )(
        normed_hidden_input[0],
        frozen_query_base[0],
        key_head_states[0],
        value_head_states[0],
        output_gradient[0],
        meta,
        adapter_down_weight[0],
        adapter_up_weight[0],
        sequence_adapter_list,
    )
    attention, key_grad, value_grad, down_grad, up_grad = pl.pallas_call(
        hand_over_kernel,
        name="hand_over",
        out_shape=tuple(
            shape(array.shape, array.dtype)
            for array in (attention, key_grad, value_grad, down_grad, up_grad)
        ),
        in_specs=[vmem()] * 5,
        out_specs=(vmem(),) * 5,
    )(attention, key_grad, value_grad, down_grad, up_grad)
    return (
        attention[None],
        key_grad[None],
        value_grad[None],
        down_grad[None],
        up_grad[None],
    )


def solution(mesh):
    in_specs = (
        P("seq", "ctx", None),
        P("seq", "ctx", None),
        P("seq", "ctx", None),
        P("seq", "ctx", None),
        P("seq", "ctx"),
        P("seq", "ctx"),
        P(),
        P("seq", None, "ctx"),
        P("seq", None, "ctx"),
        P("seq", "ctx", None),
    )
    out_specs = (
        P("seq", "ctx", None),
        P("seq", "ctx", None),
        P("seq", "ctx", None),
        P("seq", None, "ctx"),
        P("seq", None, "ctx"),
    )
    return jax.shard_map(
        per_device, mesh=mesh, in_specs=in_specs, out_specs=out_specs, check_vma=False
    )
```
